32 devices in a mesh: fourier: 4 (over y, core), meridian: 8 (over z, x).
Axes of the slice: x: 2, y: 2, z: 4, core: 2. Of those that a mesh axis runs over, the one named last changes fastest.
Arguments:
- forward_now: float32 [3, 1056, 2048], P(None, 'meridian', 'fourier'), may hold values from -3 to 3
- forward_last: float32 [3, 1056, 2048], P(None, 'meridian', 'fourier'), may hold values from -3 to 3
- adjoint_now: float32 [3, 1056, 2048], P(None, 'meridian', 'fourier'), may hold values from -3 to 3
- adjoint_last: float32 [3, 1056, 2048], P(None, 'meridian', 'fourier'), may hold values from -3 to 3
- moduli: float32 [21, 17, 8, 400], P(None, None, 'meridian', 'fourier'), may hold values from -1.8 to 1.8
- inv_radius: float32 [3200], P('meridian'), may hold values from 0.0009765625 to 0.0078125
- inv_mass: float32 [2112], P('meridian'), may hold values from 0.005 to 0.05
Outputs:
- forward_next: float32 [3, 1056, 2048], P(None, 'meridian', 'fourier')
- adjoint_next: float32 [3, 1056, 2048], P(None, 'meridian', 'fourier')
- kernel: float32 [21, 17, 8, 400], P(None, None, 'meridian', 'fourier')
The draws below stay inside these ranges and needn't reach their ends.
All inputs are finite; a program needn't handle non-finite values.
Results may differ from the reference program's by a relative error of at most 0.0001.
Values sent between devices are 32-bit elements; how exact they have to be, the bound alone decides.
A program may use at most 128 MiB of HBM per device.

```python
import math
import jax
import jax.numpy as jnp
import numpy as np
from jax import lax

F = 1024
ORD = 8
EB = 8
EA = 2
BASIS = 17
SLICES = 8
NPTS = 2112
Q = 400
NQ = 3200
N_MERIDIAN = 8


def block_levels(stream_key, dims, pieces, least, top_value):
    loudness, own = 1.0, jax.random.fold_in(stream_key, 6)
    for axis_at, parts in pieces:
        draws = jnp.exp(jax.random.uniform(jax.random.fold_in(own, axis_at), (parts,), jnp.float32, least / len(pieces), top_value / len(pieces)))
        loudness = loudness * jnp.repeat(draws, dims[axis_at] // parts).reshape([-1 if axis == axis_at else 1 for axis in range(len(dims))])
    return loudness


def normal_values(own_key, shape, spread, reach, shards=(), kind=jnp.bfloat16):
    gain = block_levels(own_key, shape, shards, -0.22, 0.18) if shards else 1.0
    drawn = jax.random.normal(own_key, shape, jnp.float32) * spread * gain
    return jnp.minimum(jnp.maximum(drawn, -reach), reach).astype(kind)


def setup_inputs(seed: int = 0) -> dict:
    key_of = jax.random.split(jax.random.key(seed), 8)
    forward_now = normal_values(key_of[0], (3, NPTS // 2, 2 * F), 0.5, 3.0, ((1, 8), (2, 4)), jnp.float32)
    forward_last = normal_values(key_of[1], (3, NPTS // 2, 2 * F), 0.5, 3.0, ((1, 8), (2, 4)), jnp.float32)
    adjoint_now = normal_values(key_of[2], (3, NPTS // 2, 2 * F), 0.5, 3.0, ((1, 8), (2, 4)), jnp.float32)
    adjoint_last = normal_values(key_of[3], (3, NPTS // 2, 2 * F), 0.5, 3.0, ((1, 8), (2, 4)), jnp.float32)
    moduli = normal_values(key_of[4], (21, BASIS, SLICES, Q), 0.3, 1.8, ((2, 8), (3, 4)), jnp.float32)
    inv_radius = jnp.clip(jnp.exp(math.log(0.0078125) - 2.0794415 * jax.random.uniform(key_of[5], (NQ,), jnp.float32) ** block_levels(key_of[5], (NQ,), ((0, 8),), -0.2, 0.2)), 0.0009765625, 0.0078125)
    inv_mass = jnp.clip(jnp.exp(math.log(0.05) - 2.3025851 * jax.random.uniform(key_of[6], (NPTS,), jnp.float32) ** block_levels(key_of[6], (NPTS,), ((0, 8),), -0.2, 0.2)), 0.005, 0.05)
    return {"forward_now": forward_now, "forward_last": forward_last, "adjoint_now": adjoint_now, "adjoint_last": adjoint_last, "moduli": moduli, "inv_radius": inv_radius, "inv_mass": inv_mass}


highest = lax.Precision.HIGHEST
kernel_weight = 0.0001

def unpack_points(values):
    shape = values.shape
    evens = values[:, :, 0::2]
    odds = values[:, :, 1::2]
    return jnp.stack([evens, odds], axis=2).reshape(shape[0], 2 * shape[1], shape[2] // 2)

def pack_points(values):
    shape = values.shape
    paired = values.reshape(shape[0], shape[1] // 2, 2, shape[2])
    packed = jnp.zeros((shape[0], shape[1] // 2, 2 * shape[2]), values.dtype)
    packed = packed.at[:, :, 0::2].set(paired[:, :, 0])
    return packed.at[:, :, 1::2].set(paired[:, :, 1])

def gll_tables():
    points_x = np.array([-1.0, -math.sqrt(3.0 / 7.0), 0.0, math.sqrt(3.0 / 7.0), 1.0])
    weights = np.array([0.1, 49.0 / 90.0, 32.0 / 45.0, 49.0 / 90.0, 0.1])
    factor = np.array([np.prod([points_x[row_at] - points_x[column] for column in range(5) if column != row_at]) for row_at in range(5)])
    derive = np.zeros((5, 5))
    for row_at in range(5):
        for col_at in range(5):
            if row_at != col_at:
                derive[row_at, col_at] = factor[row_at] / (factor[col_at] * (points_x[row_at] - points_x[col_at]))
            else:
                derive[row_at, col_at] = sum((1.0 / (points_x[row_at] - points_x[column]) for column in range(5) if column != row_at))
    return (jnp.asarray(derive, jnp.float32), jnp.asarray(np.outer(weights, weights).reshape(25), jnp.float32))

def sample_table(count):
    sample_ids = jnp.arange(count, dtype=jnp.int32)
    orders = jnp.where(sample_ids == 1, count // 2, sample_ids // 2).astype(jnp.int32)
    phases = sample_ids[:, None] * orders[None, :] % count
    angles = phases.astype(jnp.float32) * (2.0 * math.pi / count)
    sine_cols = (sample_ids % 2 == 1) & (sample_ids != 1)
    return jnp.where(sine_cols[None, :], jnp.sin(angles), jnp.cos(angles))

def basis_table(count, degree):
    sample_ids = jnp.arange(count, dtype=jnp.int32)
    column = jnp.arange(2 * degree + 1, dtype=jnp.int32)
    orders = (column + 1) // 2
    phases = sample_ids[:, None] * orders[None, :] % count
    angles = phases.astype(jnp.float32) * (2.0 * math.pi / count)
    sine_cols = (column % 2 == 0) & (column > 0)
    return jnp.where(sine_cols[None, :], jnp.sin(angles), jnp.cos(angles))

def node_weights(weights, count):
    return jnp.tile(weights, count // 25)

def to_blocks(values, count):
    width = values.shape[-1]
    leading = values[..., :4 * count, :].reshape(values.shape[:-2] + (count, 4, width))
    closing = values[..., 4::4, :][..., None, :]
    return jnp.concatenate([leading, closing], axis=-2)

def from_blocks(blocks, count):
    width = blocks.shape[-1]
    outer = blocks.shape[:-3]
    edge_pad = [(0, 0)] * len(outer)
    leading = blocks[..., :4, :].reshape(outer + (4 * count, width))
    leading = jnp.pad(leading, edge_pad + [(0, 1), (0, 0)])
    closing = jnp.pad(blocks[..., 4:, :], edge_pad + [(0, 0), (3, 0), (0, 0)])
    closing = jnp.pad(closing.reshape(outer + (4 * count, width)), edge_pad + [(1, 0), (0, 0)])
    return leading + closing

def to_elements(field, count_a, count_b):
    leads = field.shape[0]
    width = field.shape[-1]
    columns = to_blocks(field, count_b)
    columns = jnp.transpose(columns, (0, 2, 3, 1, 4))
    grid_blocks = to_blocks(columns, count_a)
    grid_blocks = jnp.transpose(grid_blocks, (0, 3, 1, 4, 2, 5))
    return grid_blocks.reshape(leads, count_a * count_b, 5, 5, width)

def from_elements(elements, count_a, count_b):
    leads = elements.shape[0]
    width = elements.shape[-1]
    grid_blocks = elements.reshape(leads, count_a, count_b, 5, 5, width)
    grid_blocks = jnp.transpose(grid_blocks, (0, 2, 4, 1, 3, 5))
    row_sums = from_blocks(grid_blocks, count_a)
    row_sums = jnp.transpose(row_sums, (0, 3, 1, 2, 4))
    return from_blocks(row_sums, count_b)

def azimuth(values, orders):
    orders_each = jnp.repeat(orders, 2)
    positions = jnp.arange(values.shape[-1], dtype=jnp.int32)
    is_even = positions % 2 == 0
    following = jnp.roll(values, -1, axis=-1)
    preceding = jnp.roll(values, 1, axis=-1)
    return jnp.where(is_even, orders_each * following, -orders_each * preceding)

def strains(displace, radius, orders, derive):
    along_a = jnp.einsum('ik,lcekjn->lceijn', derive, displace, precision=highest)
    along_b = jnp.einsum('jk,lceikn->lceijn', derive, displace, precision=highest)
    beside_all = radius[..., None] * azimuth(displace, orders)
    return jnp.stack([along_a[:, 0], along_b[:, 1], beside_all[:, 2], along_b[:, 2] + beside_all[:, 1], along_a[:, 2] + beside_all[:, 0], along_a[:, 1] + along_b[:, 0]], axis=1)

def forces(stress, radius, orders, derive):
    part_a = jnp.stack([stress[:, 0], stress[:, 5], stress[:, 4]], axis=1)
    part_b = jnp.stack([stress[:, 5], stress[:, 1], stress[:, 3]], axis=1)
    part_p = jnp.stack([stress[:, 4], stress[:, 3], stress[:, 2]], axis=1)
    from_a = jnp.einsum('ki,lcekjn->lceijn', derive, part_a, precision=highest)
    from_b = jnp.einsum('kj,lceikn->lceijn', derive, part_b, precision=highest)
    return from_a + from_b - azimuth(radius[..., None] * part_p, orders)

def voigt_index(left_at, right_at):
    lesser = min(left_at, right_at)
    larger = max(left_at, right_at)
    return lesser * 6 - lesser * (lesser - 1) // 2 + larger - lesser

def stress_samples(strain, moduli_s, dft_table, weights_q):
    sampled = jnp.dot(strain, dft_table.T, precision=highest)
    stress_list = []
    for left_at in range(6):
        total = moduli_s[voigt_index(left_at, 0)] * sampled[:, 0]
        for right_at in range(1, 6):
            total = total + moduli_s[voigt_index(left_at, right_at)] * sampled[:, right_at]
        stress_list.append(total)
    weighted = jnp.stack(stress_list, axis=1) * weights_q[:, None]
    coeffs = jnp.dot(weighted, dft_table, precision=highest) / dft_table.shape[0]
    return (coeffs, sampled)

def kernel_terms(sampled, basis_rows, weights_q):
    forward_s = sampled[0]
    adjoint_s = sampled[1]
    terms = []
    for left_at in range(6):
        for right_at in range(left_at, 6):
            if left_at == right_at:
                terms.append(forward_s[left_at] * adjoint_s[left_at])
            else:
                terms.append(forward_s[left_at] * adjoint_s[right_at] + forward_s[right_at] * adjoint_s[left_at])
    stacked = jnp.stack(terms) * weights_q[:, None]
    projected = jnp.dot(stacked, basis_rows, precision=highest)
    return jnp.transpose(projected, (0, 2, 1)) * kernel_weight

def reference(forward_now, forward_last, adjoint_now, adjoint_last, moduli, inv_radius, inv_mass):
    forward_now = unpack_points(forward_now)
    forward_last = unpack_points(forward_last)
    adjoint_now = unpack_points(adjoint_now)
    adjoint_last = unpack_points(adjoint_last)
    derive, weights = gll_tables()
    width_b = 4 * EB + 1
    row_count = 4 * EA
    nodes_slice = 25 * EA * EB
    fields = jnp.stack([forward_now, adjoint_now]).reshape(2, 3, row_count * N_MERIDIAN, width_b, F)
    padded = jnp.pad(fields, ((0, 0), (0, 0), (0, 1), (0, 0), (0, 0)))
    dft_table = sample_table(F)
    basis_rows = basis_table(F, ORD)
    orders_full = jnp.arange(F // 2, dtype=jnp.int32).astype(jnp.float32)
    weights_q = node_weights(weights, nodes_slice)

    def one_slice(slice_at):
        block = lax.dynamic_slice_in_dim(padded, slice_at * row_count, row_count + 1, axis=2)
        block = block.reshape(6, row_count + 1, width_b, F)
        elements = to_elements(block, EA, EB).reshape(2, 3, EA * EB, 5, 5, F)
        radius = lax.dynamic_slice_in_dim(inv_radius, slice_at * nodes_slice, nodes_slice).reshape(EA * EB, 5, 5)
        moduli_m = lax.dynamic_index_in_dim(moduli, slice_at, axis=2, keepdims=False)
        moduli_s = jnp.einsum('cjq,nj->cqn', moduli_m, basis_rows, precision=highest)
        strain = strains(elements, radius, orders_full, derive).reshape(2, 6, nodes_slice, F)
        coeffs, sampled = stress_samples(strain, moduli_s, dft_table, weights_q)
        pushed = forces(coeffs.reshape(2, 6, EA * EB, 5, 5, F), radius, orders_full, derive)
        assembled = from_elements(pushed.reshape(6, EA * EB, 5, 5, F), EA, EB)
        return (assembled, kernel_terms(sampled, basis_rows, weights_q))
    assembled, kernel = lax.map(one_slice, jnp.arange(N_MERIDIAN, dtype=jnp.int32))
    own_rows = assembled[:, :, :row_count]
    carried = jnp.concatenate([jnp.zeros_like(assembled[:1, :, row_count]), assembled[:-1, :, row_count]], axis=0)
    own_rows = own_rows.at[:, :, 0].add(carried)
    forces_all = jnp.transpose(own_rows, (1, 0, 2, 3, 4)).reshape(2, 3, NPTS, F)
    mass_scale = inv_mass[:, None]
    forward_next = 2.0 * forward_now - forward_last - mass_scale * forces_all[0]
    adjoint_next = 2.0 * adjoint_now - adjoint_last - mass_scale * forces_all[1]
    return (pack_points(forward_next), pack_points(adjoint_next), jnp.transpose(kernel, (1, 2, 0, 3)))
```

```python
import functools
import math

import jax
import jax.numpy as jnp
import numpy as np
from jax import lax
from jax.experimental import pallas as pl
from jax.experimental.pallas import tpu as pltpu
from jax.sharding import PartitionSpec as P

ORD = 8
EB = 8
BASIS = 2 * ORD + 1
kernel_weight = 0.0001
bf16 = jnp.bfloat16
f32 = jnp.float32
PAIRS = [(a, b) for a in range(6) for b in range(a, 6)]
PART_A, PART_B, PART_P = (0, 5, 4), (5, 1, 3), (4, 3, 2)


def gll_tables():
    x = np.array([-1.0, -math.sqrt(3.0 / 7.0), 0.0, math.sqrt(3.0 / 7.0), 1.0])
    weights = np.array([0.1, 49.0 / 90.0, 32.0 / 45.0, 49.0 / 90.0, 0.1])
    factor = np.array([np.prod([x[i] - x[k] for k in range(5) if k != i]) for i in range(5)])
    derive = np.zeros((5, 5))
    for i in range(5):
        for k in range(5):
            if i != k:
                derive[i, k] = factor[i] / (factor[k] * (x[i] - x[k]))
            else:
                derive[i, k] = sum(1.0 / (x[i] - x[o]) for o in range(5) if o != i)
    return derive, np.outer(weights, weights).reshape(25)


def sample_count(orders):
    n = orders + 2 * ORD + 1
    return n, 0 if n <= 64 else -(-(n - 64) // 128)


def place(re, im, nb):
    cut, n = 128 * nb, re.shape[1]
    rest = np.zeros((re.shape[0], 128))
    head = np.zeros((2, re.shape[0], cut))
    wide = min(n, cut)
    head[0, :, :wide], head[1, :, :wide] = re[:, :wide], im[:, :wide]
    if n > cut:
        rest[:, :n - cut], rest[:, 64:64 + n - cut] = re[:, cut:], im[:, cut:]
    return np.concatenate([head[0], head[1], rest], axis=1)


def waves(orders):
    n, nb = sample_count(orders)
    at = np.arange(-ORD, orders + ORD + 1)
    turn = 2 * np.pi * ((at[:, None] * np.arange(n)[None, :]) % n) / n
    return place(np.cos(turn), np.sin(turn), nb), place(np.sin(turn), -np.cos(turn), nb)


def with_turned(table):
    turned = np.zeros_like(table)
    turned[0::2], turned[1::2] = -table[1::2], table[0::2]
    return np.concatenate([table, turned], axis=1).astype(np.float32)


def block_tables(orders, own):
    ec, es = waves(orders)
    inner = np.zeros((own + 4 * ORD, ec.shape[1]))
    for row, p in [(2 * p, p) for p in range(orders)] + [(own + 2 * i, i - ORD) for i in range(ORD)] \
            + [(own + 2 * ORD + 2 * i, orders + i) for i in range(ORD)]:
        inner[row], inner[row + 1] = 0.5 * ec[p + ORD], 0.5 * es[p + ORD]
    first, last = np.zeros_like(inner), np.zeros_like(inner)
    first[0], first[1] = 0.5 * ec[ORD], -inner[1]
    for p in range(1, ORD + 1):
        first[2 * p] += 0.5 * ec[ORD - p]
        first[2 * p + 1] -= 0.5 * es[ORD - p]
    first[own:own + 2 * ORD] = -inner[own:own + 2 * ORD]
    last[own + 2 * ORD:] = -inner[own + 2 * ORD:]
    last[own + 2 * ORD + 1] += ec[orders + ORD]
    for j in range(1, ORD + 1):
        last[2 * (orders - j)] += 0.5 * ec[orders + j + ORD]
        last[2 * (orders - j) + 1] -= 0.5 * es[orders + j + ORD]
    halo_last = np.zeros_like(inner)
    halo_last[own + 2 * ORD + 1] = 0.5 * ec[orders + ORD]
    return [with_turned(t) for t in (inner, first, last, halo_last)]


def basis_rows(orders):
    n, nb = sample_count(orders)
    j = np.arange(BASIS)[:, None]
    turn = ((j + 1) // 2) * (2 * np.pi * np.arange(n)[None, :] / n)
    rows = np.where((j % 2 == 0) & (j > 0), np.sin(turn), np.cos(turn))
    both = place(rows, rows, nb)
    return both[:, 128 * nb:]


def split_host(values):
    wide = np.asarray(values, np.float32)
    hi = wide.astype(bf16)
    return hi, (wide - hi.astype(np.float32)).astype(bf16)


def split_device(values):
    hi = lax.reduce_precision(values, 8, 7)
    return hi.astype(bf16), (values - hi).astype(bf16)


def split(values):
    hi = values.astype(bf16)
    return hi, (values - hi.astype(f32)).astype(bf16)


def nt(a, b):
    return lax.dot_general(a, b, (((1,), (1,)), ((), ())), preferred_element_type=f32)


def nn(a, b):
    return lax.dot_general(a, b, (((1,), (0,)), ((), ())), preferred_element_type=f32)


def line(matrix, u):
    s0, d0, s1, d1 = u[0] + u[4], u[0] - u[4], u[1] + u[3], u[1] - u[3]
    out = [None] * 5
    for i in range(2):
        m = [float(v) for v in matrix[i]]
        odd = (0.5 * (m[0] - m[4])) * d0 + (0.5 * (m[1] - m[3])) * d1
        even = (0.5 * (m[0] + m[4])) * s0 + (0.5 * (m[1] + m[3])) * s1 + m[2] * u[2]
        out[i], out[4 - i] = even + odd, odd - even
    m = [float(v) for v in matrix[2]]
    out[2] = m[0] * d0 + m[1] * d1
    return out


def core(cfg, x_ref, hx_ref, mod_ref, rad_ref, fh_ref, fl_ref, ah_ref, al_ref, perm_ref, a3_ref, aa_ref, wrow_ref,
         f_ref, hb_ref, k_ref, uz, es, cs, ps, accb, s_ref, s1_ref, s2_ref, t3_ref):
    nf, own, R, wide, count_a, nodes, nb, hrow, derive = cfg
    lanes = x_ref.shape[2]
    W = 256 * nb + 128
    blocks = 2 * nb + 1
    halo = 4 * ORD
    tables = ((fh_ref, fl_ref), (ah_ref, al_ref))

    def onehot(shape, hit):
        a = lax.broadcasted_iota(jnp.int32, shape, 0)
        b = lax.broadcasted_iota(jnp.int32, shape, 1)
        return jnp.where(hit(a, b), 1.0, 0.0).astype(bf16)

    s_ref[...] = onehot((lanes, 2 * own), lambda a, b: (a % 2) * own + a // 2 == b)
    spot = lambda a: (a % 2) * 128 + (a // halo) * (2 * ORD) + (a % halo) // 2
    s1_ref[...] = onehot((128, 256), lambda a, b: (a < 2 * halo) & ((spot(a) == b) | (spot(a) + halo == b)))
    s2_ref[...] = onehot((128, 256), lambda a, b: (a < 2 * halo) & (spot(a) + 2 * halo == b))
    for l, (h, lo) in enumerate(tables):
        t3_ref[l, 0:halo] = h[own:]
        t3_ref[l, halo:2 * halo] = lo[own:]
        t3_ref[l, 2 * halo:3 * halo] = h[own:]
        t3_ref[l, 3 * halo:] = jnp.zeros((128 - 3 * halo, 2 * W), bf16)

    def moduli_step(r, carry):
        m = jnp.concatenate([mod_ref[d, r] for d in range(nf)], axis=1) * wrow_ref[0:1, :]
        h, lo = split(m)
        rows = jnp.concatenate([h, h, lo, jnp.zeros_like(h)], axis=0)
        mt = nt(perm_ref[...], rows).astype(bf16)
        cs[pl.ds(pl.multiple_of(r * nodes, 8), nodes), :] = nn(mt, a3_ref[...])
        return carry

    lax.fori_loop(0, 21, moduli_step, 0)

    for l, (h_ref, l_ref) in enumerate(tables):
        def ahead(c, carry, l=l, h_ref=h_ref, l_ref=l_ref):
            lc = 3 * l + c
            xh, xl = split(x_ref[lc])
            dh, dl = nn(xh, s_ref[...]).astype(bf16), nn(xl, s_ref[...]).astype(bf16)
            hh, hl = split(hx_ref[lc])
            he = (nn(hh, s1_ref[...]) + nn(hl, s2_ref[...])).astype(bf16)
            for par in range(2):
                ph, plo = dh[:, par * own:(par + 1) * own], dl[:, par * own:(par + 1) * own]
                at = pl.ds(pl.multiple_of((2 * lc + par) * R, 8), R)
                out = (nn(ph, h_ref[:own]) + nn(ph, l_ref[:own]) + nn(plo, h_ref[:own])
                       + nn(he[:, par * 128:(par + 1) * 128], t3_ref[l]))
                for b in range(2 * blocks):
                    uz[b, at, :] = out[:, 128 * b:128 * (b + 1)]
            return carry
        lax.fori_loop(0, 3, ahead, 0)

    def point(a, j):
        p = wide * a + j
        return p % 2, p // 2 + (hrow if a == 4 * count_a else 0)

    def strain_step(t, carry):
        l, blk = t // blocks, t % blocks
        lane = pl.multiple_of(blk * 128, 128)
        blk_z = blocks + blk

        def grid(c, ea, at_blk):
            out = []
            for i in range(5):
                row = []
                for j in range(5):
                    par, r = point(4 * ea + i, j)
                    base = (2 * (3 * l + c) + par) * R + r
                    row.append(uz[at_blk, pl.ds(base, 8, stride=2), :])
                out.append(row)
            return out

        def put(v, ea, i, j, value):
            row = pl.multiple_of((6 * l + v) * nodes + ((ea * 5 + i) * 5 + j) * 8, 8)
            es[pl.ds(row, 8), pl.ds(lane, 128)] = value

        for ea in range(count_a):
            rad = lambda i, j: rad_ref[((ea * 5 + i) * 5 + j) * 8:((ea * 5 + i) * 5 + j) * 8 + 8, :]
            cols = lambda u: [[row[j] for row in u] for j in range(5)]
            u = grid(0, ea, blk)
            for j, col in enumerate(cols(u)):
                for i, v in enumerate(line(derive, col)):
                    put(0, ea, i, j, v)
            shear = [line(derive, row) for row in u]
            u = grid(1, ea, blk)
            for j, col in enumerate(cols(u)):
                for i, v in enumerate(line(derive, col)):
                    put(5, ea, i, j, v + shear[i][j])
            for i, row in enumerate(u):
                for j, v in enumerate(line(derive, row)):
                    put(1, ea, i, j, v)
            u = grid(2, ea, blk)
            z = grid(0, ea, blk_z)
            for j, col in enumerate(cols(u)):
                for i, v in enumerate(line(derive, col)):
                    put(4, ea, i, j, v + rad(i, j) * z[i][j])
            z = grid(1, ea, blk_z)
            for i, row in enumerate(u):
                for j, v in enumerate(line(derive, row)):
                    put(3, ea, i, j, v + rad(i, j) * z[i][j])
            z = grid(2, ea, blk_z)
            for i in range(5):
                for j in range(5):
                    put(2, ea, i, j, rad(i, j) * z[i][j])
        return carry

    lax.fori_loop(0, 2 * blocks, strain_step, 0)

    def node_step(t, carry):
        row = pl.multiple_of(t * 8, 8)
        at = lambda v: pl.ds(pl.multiple_of(v * nodes + row, 8), 8)

        def one(c_lane, e_lane, prods):
            ce, el = slice(c_lane, c_lane + 128), slice(e_lane, e_lane + 128)
            fw = [es[at(v), el] for v in range(6)]
            ad = [es[at(6 + v), el] for v in range(6)]
            sf, sa = [None] * 6, [None] * 6

            def add(sums, v, term):
                sums[v] = term if sums[v] is None else sums[v] + term

            out = []
            for r, (v, w) in enumerate(PAIRS):
                c = cs[at(r), ce]
                add(sf, v, c * fw[w])
                add(sa, v, c * ad[w])
                if v != w:
                    add(sf, w, c * fw[v])
                    add(sa, w, c * ad[v])
                    prod = fw[v] * ad[w] + fw[w] * ad[v]
                else:
                    prod = fw[v] * ad[v]
                if prods is not None:
                    ps[at(r), ce] = ps[at(r), ce] + prod
                else:
                    ps[at(r), ce] = prod
            for v in range(6):
                es[at(v), el] = sf[v]
                es[at(6 + v), el] = sa[v]
            return out

        for b in range(nb):
            one(128 * b, 128 * b, None)
            one(128 * b, 128 * (nb + b), True)
        one(128 * nb, 256 * nb, None)
        return carry

    lax.fori_loop(0, nodes // 8, node_step, 0)

    def project_step(r, carry):
        ph, plo = split(ps[pl.ds(pl.multiple_of(r * nodes, 8), nodes), :])
        first = nt(aa_ref[...], ph)
        accb[r] = first[:32] + first[32:] + nt(aa_ref[:32], plo)
        return carry

    lax.fori_loop(0, 21, project_step, 0)

    def force_step(t, carry):
        l, blk = t // blocks, t % blocks
        lane = pl.multiple_of(blk * 128, 128)
        blk_z = blocks + blk
        top = lax.broadcasted_iota(jnp.int32, (8, 128), 0) == 0

        def get(v, ea, i, j):
            row = pl.multiple_of((6 * l + v) * nodes + ((ea * 5 + i) * 5 + j) * 8, 8)
            return es[pl.ds(row, 8), pl.ds(lane, 128)]

        def store(c, a, row, at_blk):
            def where(j):
                par, r = point(a, j)
                return (2 * (3 * l + c) + par) * R + r
            for j in range(1, 4):
                uz[at_blk, pl.ds(where(j), 8, stride=2), :] = row[j]
            back = pltpu.roll(row[4], 1, 0)
            uz[at_blk, pl.ds(where(0), 8, stride=2), :] = row[0] + jnp.where(top, 0.0, back)
            uz[at_blk, pl.ds(where(4) + 14, 1), :] = row[4][7:8]

        last = wide * (4 * count_a + 1)
        for c in range(3):
            held, held_z = None, None
            spare = (2 * (3 * l + c) + last % 2) * R + last // 2 + hrow
            for b in (blk, blk_z):
                uz[b, pl.ds(spare, 1), :] = jnp.zeros((1, 128), f32)
            for ea in range(count_a):
                rad = lambda i, j: rad_ref[((ea * 5 + i) * 5 + j) * 8:((ea * 5 + i) * 5 + j) * 8 + 8, :]
                cols = [line(derive.T, [get(PART_A[c], ea, i, j) for i in range(5)]) for j in range(5)]
                for i in range(5):
                    row = line(derive.T, [get(PART_B[c], ea, i, j) for j in range(5)])
                    row = [row[j] + cols[j][i] for j in range(5)]
                    row_z = [rad(i, j) * get(PART_P[c], ea, i, j) for j in range(5)]
                    if i == 0 and held is not None:
                        row = [p + q for p, q in zip(row, held)]
                        row_z = [p + q for p, q in zip(row_z, held_z)]
                    if i == 4 and ea + 1 < count_a:
                        held, held_z = row, row_z
                    else:
                        store(c, 4 * ea + i, row, blk)
                        store(c, 4 * ea + i, row_z, blk_z)
        return carry

    lax.fori_loop(0, 2 * blocks, force_step, 0)

    for l in range(2):
        h_ref, l_ref = tables[1 - l]

        def back(c, carry, l=l, h_ref=h_ref, l_ref=l_ref):
            lc = 3 * l + c
            both, edge_h, edge_l = [], [], []
            for par in range(2):
                at = pl.ds(pl.multiple_of((2 * lc + par) * R, 8), R)
                h, lo = split(jnp.concatenate([uz[b, at, :] for b in range(2 * blocks)], axis=1))
                both.append(nt(h, h_ref[:own]) + nt(h, l_ref[:own]) + nt(lo, h_ref[:own]))
                edge_h.append(nt(h, t3_ref[1 - l]))
                edge_l.append(nt(lo, t3_ref[1 - l]))
            h, lo = split(jnp.concatenate(both, axis=1))
            f_ref[lc] = nt(h, s_ref[...]) + nt(lo, s_ref[...])
            h, lo = split(jnp.concatenate(edge_h, axis=1))
            edge = nt(h, s1_ref[...]) + nt(lo, s1_ref[...])
            h, lo = split(jnp.concatenate(edge_l, axis=1))
            hb_ref[lc] = edge + nt(h, s2_ref[...]) + nt(lo, s2_ref[...])
            return carry
        lax.fori_loop(0, 3, back, 0)

    acc = accb[...].reshape(21 * 32, nodes)
    h, lo = split(acc)
    k_ref[...] = (nn(h, perm_ref[...]) + nn(lo, perm_ref[...])).reshape(k_ref.shape)


def body(forward_now, forward_last, adjoint_now, adjoint_last, moduli, inv_radius, inv_mass):
    derive, weights = gll_tables()
    wide = 4 * EB + 1
    nf = lax.axis_size("fourier")
    nm = lax.axis_size("meridian")
    me = lax.axis_index("fourier")
    comps, rows, lanes = forward_now.shape
    local = lanes // 2
    total = local * nf
    orders = local // 2
    own = -(-local // 128) * 128
    row_count = 2 * rows // wide
    count_a = row_count // 4
    nodes_mine = moduli.shape[3]
    nodes = nodes_mine * nf
    edge = (wide + 1) // 2
    start = -(-rows // 8) * 8
    R = -(-(start + edge) // 16) * 16
    n, nb = sample_count(orders)
    W = 256 * nb + 128
    halo = 4 * ORD

    packed = jnp.concatenate([forward_now, adjoint_now], axis=0)
    below = [(i + 1, i) for i in range(nm - 1)]
    above = [(i, i + 1) for i in range(nm - 1)]
    upper = lax.ppermute(packed[:, :edge], "meridian", below)
    packed = jnp.concatenate([jnp.pad(packed, ((0, 0), (0, start - rows), (0, 0))),
                              jnp.pad(upper, ((0, 0), (0, R - start - edge), (0, 0)))], axis=1)
    ring_up = [(i, (i + 1) % nf) for i in range(nf)]
    ring_down = [((i + 1) % nf, i) for i in range(nf)]
    low = lax.ppermute(packed[:, :, lanes - halo:], "fourier", ring_up)
    up = lax.ppermute(packed[:, :, :halo], "fourier", ring_down)
    hx = jnp.pad(jnp.concatenate([low, up], axis=2), ((0, 0), (0, 0), (0, 128 - 2 * halo)))
    mods = jnp.broadcast_to(moduli[None, :, :, 0, :], (nf, 21, BASIS, nodes_mine))
    mods = lax.all_to_all(mods, "fourier", split_axis=0, concat_axis=0, tiled=True)
    mods = jnp.pad(mods, ((0, 0), (0, 0), (0, 32 - BASIS), (0, 128 - nodes_mine)))

    inner, first, last, halo_last = block_tables(orders, own)
    is_first = jnp.where(me == 0, 1.0, 0.0).astype(f32)
    is_last = jnp.where(me == nf - 1, 1.0, 0.0).astype(f32)
    head, tail = 24, slice(local - 2 * ORD, local)
    row = np.arange(own + halo)
    at_order = np.where(row < own, row // 2, np.where(row < own + 2 * ORD, (row - own) // 2 - ORD,
                                                      orders + (row - own - 2 * ORD) // 2))
    nyquist = (row // 2) == (own + 2 * ORD) // 2
    turn = jnp.asarray(at_order, f32) + (me * orders).astype(f32)
    turn = turn * (1.0 - jnp.asarray(nyquist, f32) * is_last)
    scale = jnp.concatenate([jnp.ones((own + halo, W), f32), jnp.broadcast_to(turn[:, None], (own + halo, W))], axis=1)
    fix_turned = with_turned(np.where(np.arange(head)[:, None] == 1, -inner[:head, :W], 0.0).astype(np.float32))
    parts_a = [inner[:head] + is_first * first[:head], inner[head:local - 2 * ORD] * jnp.ones((1, 1), f32),
               inner[tail] + is_last * last[tail], jnp.asarray(inner[local:own]),
               inner[own:] + is_first * first[own:] + is_last * last[own:]]
    parts_f = [inner[:head] + is_first * fix_turned, parts_a[1], jnp.asarray(inner[tail]), parts_a[3],
               is_last * halo_last[own:]]
    fh, fl = split_device(jnp.concatenate(parts_f, axis=0) * scale)
    ah, al = split_device(jnp.concatenate(parts_a, axis=0) * scale)

    rows_a = basis_rows(orders)
    bh, bl = split_host(rows_a)
    a3 = np.zeros((128, rows_a.shape[1]), bf16)
    a3[0:BASIS], a3[32:32 + BASIS], a3[64:64 + BASIS] = bh, bl, bh
    aa = np.zeros((64, rows_a.shape[1]), bf16)
    aa[0:BASIS], aa[32:32 + BASIS] = bh, bl
    perm = np.zeros((nodes, nf * 128), np.float32)
    wrow = np.zeros((8, nf * 128), np.float32)
    for ea in range(count_a):
        for eb in range(EB):
            for ij in range(25):
                q = (ea * EB + eb) * 25 + ij
                spot = (q // nodes_mine) * 128 + q % nodes_mine
                perm[(ea * 25 + ij) * EB + eb, spot] = 1.0
                wrow[:, spot] = weights[ij]
    radius = jnp.transpose(inv_radius.reshape(count_a, EB, 25), (0, 2, 1)).reshape(nodes, 1)
    radius = jnp.broadcast_to(radius, (nodes, 128))

    cfg = (nf, own, R, wide, count_a, nodes, nb, start - rows, derive)
    vmem = pl.BlockSpec(memory_space=pltpu.VMEM)
    CW = rows_a.shape[1]
    force, spill, acc = pl.pallas_call(
        functools.partial(core, cfg),
        out_shape=(jax.ShapeDtypeStruct((2 * comps, R, lanes), f32),
                   jax.ShapeDtypeStruct((2 * comps, R, 128), f32),
                   jax.ShapeDtypeStruct((21, 32, nf * 128), f32)),
        in_specs=[vmem] * 12,
        out_specs=(vmem, vmem, vmem),
        scratch_shapes=[pltpu.VMEM((2 * W // 128, 4 * comps * R, 128), f32), pltpu.VMEM((12 * nodes, W), f32),
                        pltpu.VMEM((21 * nodes, CW), f32), pltpu.VMEM((21 * nodes, CW), f32),
                        pltpu.VMEM((21, 32, nodes), f32), pltpu.VMEM((lanes, 2 * own), bf16),
                        pltpu.VMEM((128, 256), bf16), pltpu.VMEM((128, 256), bf16),
                        pltpu.VMEM((2, 128, 2 * W), bf16)],
        compiler_params=pltpu.CompilerParams(vmem_limit_bytes=60 * 1024 * 1024),
    )(packed, hx, mods, radius, fh, fl, ah, al, jnp.asarray(perm.astype(bf16)), jnp.asarray(a3), jnp.asarray(aa),
      jnp.asarray(wrow * (2.0 / n)))

    to_up = lax.ppermute(spill[:, :, halo:2 * halo], "fourier", ring_up)
    to_low = lax.ppermute(spill[:, :, :halo], "fourier", ring_down)
    force = force + jnp.pad(to_up, ((0, 0), (0, 0), (0, lanes - halo)))
    force = force + jnp.pad(to_low, ((0, 0), (0, 0), (lanes - halo, 0)))
    carried = lax.ppermute(force[:, start:start + edge], "meridian", above)
    force = force[:, :rows] + jnp.pad(carried, ((0, 0), (0, rows - edge), (0, 0)))
    mass = inv_mass.reshape(rows, 2)
    is_even = lax.broadcasted_iota(jnp.int32, (rows, lanes), 1) % 2 == 0
    mass = jnp.where(is_even, mass[:, :1], mass[:, 1:])
    forward_next = 2.0 * forward_now - forward_last - mass * force[:comps]
    adjoint_next = 2.0 * adjoint_now - adjoint_last - mass * force[comps:]
    sums = acc.reshape(21, 32, nf, 128)[:, :BASIS, :, :nodes_mine]
    sums = jnp.transpose(sums, (2, 0, 1, 3))
    sums = lax.all_to_all(sums, "fourier", split_axis=0, concat_axis=0, tiled=True).sum(axis=0)
    wq = np.tile(weights, nodes_mine // 25) * (kernel_weight * 2.0 * total / n)
    return (forward_next, adjoint_next, (sums * jnp.asarray(wq, f32))[:, :, None, :])


def solution(mesh):
    field = P(None, "meridian", "fourier")
    grid = P(None, None, "meridian", "fourier")
    in_specs = (field, field, field, field, grid, P("meridian"), P("meridian"))
    return jax.shard_map(body, mesh=mesh, in_specs=in_specs, out_specs=(field, field, grid),
                         check_vma=False)
```

```python
import functools
import math

import jax
import jax.numpy as jnp
import numpy as np
from jax import lax
from jax.experimental import pallas as pl
from jax.experimental.pallas import tpu as pltpu
from jax.sharding import PartitionSpec as P

ORD = 8
EB = 8
BASIS = 2 * ORD + 1
HR = (4 * EB + 2) // 2 // 8 * 8 + 8
MESH = pl.DeviceIdType.MESH
kernel_weight = 0.0001
bf16 = jnp.bfloat16
f32 = jnp.float32
PAIRS = [(a, b) for a in range(6) for b in range(a, 6)]
PART_A, PART_B, PART_P = (0, 5, 4), (5, 1, 3), (4, 3, 2)


def gll_tables():
    x = np.array([-1.0, -math.sqrt(3.0 / 7.0), 0.0, math.sqrt(3.0 / 7.0), 1.0])
    weights = np.array([0.1, 49.0 / 90.0, 32.0 / 45.0, 49.0 / 90.0, 0.1])
    factor = np.array([np.prod([x[i] - x[k] for k in range(5) if k != i]) for i in range(5)])
    derive = np.zeros((5, 5))
    for i in range(5):
        for k in range(5):
            if i != k:
                derive[i, k] = factor[i] / (factor[k] * (x[i] - x[k]))
            else:
                derive[i, k] = sum(1.0 / (x[i] - x[o]) for o in range(5) if o != i)
    return derive, np.outer(weights, weights).reshape(25)


def sample_count(orders):
    n = orders + 2 * ORD + 1
    return n, 0 if n <= 64 else -(-(n - 64) // 128)


def place(re, im, nb):
    cut, n = 128 * nb, re.shape[1]
    rest = np.zeros((re.shape[0], 128))
    head = np.zeros((2, re.shape[0], cut))
    wide = min(n, cut)
    head[0, :, :wide], head[1, :, :wide] = re[:, :wide], im[:, :wide]
    if n > cut:
        rest[:, :n - cut], rest[:, 64:64 + n - cut] = re[:, cut:], im[:, cut:]
    return np.concatenate([head[0], head[1], rest], axis=1)


def waves(orders):
    n, nb = sample_count(orders)
    at = np.arange(-ORD, orders + ORD + 1)
    turn = 2 * np.pi * ((at[:, None] * np.arange(n)[None, :]) % n) / n
    return place(np.cos(turn), np.sin(turn), nb), place(np.sin(turn), -np.cos(turn), nb)


def with_turned(table):
    turned = np.zeros_like(table)
    turned[0::2], turned[1::2] = -table[1::2], table[0::2]
    return np.concatenate([table, turned], axis=1).astype(np.float32)


def block_tables(orders, own):
    ec, es = waves(orders)
    inner = np.zeros((own + 4 * ORD, ec.shape[1]))
    for row, p in [(2 * p, p) for p in range(orders)] + [(own + 2 * i, i - ORD) for i in range(ORD)] \
            + [(own + 2 * ORD + 2 * i, orders + i) for i in range(ORD)]:
        inner[row], inner[row + 1] = 0.5 * ec[p + ORD], 0.5 * es[p + ORD]
    first, last = np.zeros_like(inner), np.zeros_like(inner)
    first[0], first[1] = 0.5 * ec[ORD], -inner[1]
    for p in range(1, ORD + 1):
        first[2 * p] += 0.5 * ec[ORD - p]
        first[2 * p + 1] -= 0.5 * es[ORD - p]
    first[own:own + 2 * ORD] = -inner[own:own + 2 * ORD]
    last[own + 2 * ORD:] = -inner[own + 2 * ORD:]
    last[own + 2 * ORD + 1] += ec[orders + ORD]
    for j in range(1, ORD + 1):
        last[2 * (orders - j)] += 0.5 * ec[orders + j + ORD]
        last[2 * (orders - j) + 1] -= 0.5 * es[orders + j + ORD]
    halo_last = np.zeros_like(inner)
    halo_last[own + 2 * ORD + 1] = 0.5 * ec[orders + ORD]
    return [with_turned(t) for t in (inner, first, last, halo_last)]


def basis_rows(orders):
    n, nb = sample_count(orders)
    j = np.arange(BASIS)[:, None]
    turn = ((j + 1) // 2) * (2 * np.pi * np.arange(n)[None, :] / n)
    rows = np.where((j % 2 == 0) & (j > 0), np.sin(turn), np.cos(turn))
    both = place(rows, rows, nb)
    return both[:, 128 * nb:]


def split_host(values):
    wide = np.asarray(values, np.float32)
    hi = wide.astype(bf16)
    return hi, (wide - hi.astype(np.float32)).astype(bf16)


def split_device(values):
    hi = lax.reduce_precision(values, 8, 7)
    return hi.astype(bf16), (values - hi).astype(bf16)


def split(values):
    hi = values.astype(bf16)
    return hi, (values - hi.astype(f32)).astype(bf16)


def nt(a, b):
    return lax.dot_general(a, b, (((1,), (1,)), ((), ())), preferred_element_type=f32)


def nn(a, b):
    return lax.dot_general(a, b, (((1,), (0,)), ((), ())), preferred_element_type=f32)


def line(matrix, u):
    s0, d0, s1, d1 = u[0] + u[4], u[0] - u[4], u[1] + u[3], u[1] - u[3]
    out = [None] * 5
    for i in range(2):
        m = [float(v) for v in matrix[i]]
        odd = (0.5 * (m[0] - m[4])) * d0 + (0.5 * (m[1] - m[3])) * d1
        even = (0.5 * (m[0] + m[4])) * s0 + (0.5 * (m[1] + m[3])) * s1 + m[2] * u[2]
        out[i], out[4 - i] = even + odd, odd - even
    m = [float(v) for v in matrix[2]]
    out[2] = m[0] * d0 + m[1] * d1
    return out


def core(cfg, fn_ref, fo_ref, an_ref, ao_ref, mod_ref, rad_ref, mass_ref, fh_ref, fl_ref, ah_ref, al_ref, perm_ref,
         a3_ref, aa_ref, wrow_ref, krow_ref, nyq_ref, f_ref, a_ref, k_ref,
         uz, es, cs, ps, accb, s_ref, s1_ref, s2_ref, t3_ref, xb, last, modr, modx, rh, stage, ring, force,
         edge_f, rm, spill, rspill, kb, kr, lsem, ssem, rsem):
    nf, nm, own, R, wide, count_a, nodes, nb, hrow, edge, derive = cfg
    rows, lanes = fn_ref.shape[1:]
    W = 256 * nb + 128
    blocks = 2 * nb + 1
    halo = 4 * ORD
    main = R - HR
    tables = ((fh_ref, fl_ref), (ah_ref, al_ref))
    me, mi = lax.axis_index("fourier"), lax.axis_index("meridian")
    up, down = lax.rem(me + 1, nf), lax.rem(me + nf - 1, nf)
    has_prev, has_next = mi > 0, mi < nm - 1
    is_last = jnp.where(me == nf - 1, 1.0, 0.0).astype(f32)

    def remote(src, dst, at, meridian, fourier):
        return pltpu.make_async_remote_copy(
            src_ref=src, dst_ref=dst, send_sem=ssem.at[at], recv_sem=rsem.at[at],
            device_id={"meridian": meridian, "fourier": fourier}, device_id_type=MESH)

    first = pl.ds(0, HR)
    body_rows, tail_rows = pl.ds(0, main), pl.ds(main, HR)
    prev, nxt = mi - 1, mi + 1
    to_prev = [remote(fn_ref.at[:, first], rh.at[0:3], 0, prev, me),
               remote(an_ref.at[:, first], rh.at[3:6], 1, prev, me),
               remote(stage.at[0, first], ring.at[0, tail_rows], 2, prev, down),
               remote(stage.at[1, first], ring.at[1, tail_rows], 3, prev, up)]
    to_ring = [remote(stage.at[0], ring.at[0, body_rows], 4, mi, down),
               remote(stage.at[1], ring.at[1, body_rows], 5, mi, up)]
    to_next = [remote(edge_f, rm, 6, nxt, me),
               remote(spill.at[0, tail_rows], rspill.at[0, tail_rows], 7, nxt, down),
               remote(spill.at[1, tail_rows], rspill.at[1, tail_rows], 8, nxt, up)]
    to_spill = [remote(spill.at[0, body_rows], rspill.at[0, body_rows], 9, mi, down),
                remote(spill.at[1, body_rows], rspill.at[1, body_rows], 10, mi, up)]
    mod_send = [remote(mod_ref, modr.at[me], 11 + s, mi, lax.rem(me + s + 1, nf)) for s in range(nf - 1)]
    mod_recv = [remote(mod_ref, modr.at[lax.rem(me + nf - 1 - s, nf)], 11 + s, mi, me) for s in range(nf - 1)]
    base = 11 + nf - 1
    k_send = [remote(kb.at[lax.rem(me + s + 1, nf)], kr.at[s], base + s, mi, lax.rem(me + s + 1, nf))
              for s in range(nf - 1)]

    barrier = pltpu.get_barrier_semaphore()

    def greet(meridian, fourier):
        pl.semaphore_signal(barrier, inc=1, device_id={"meridian": meridian, "fourier": fourier},
                            device_id_type=MESH)

    for s in range(1, nf):
        greet(mi, lax.rem(me + s, nf))
    for there, other in ((has_prev, prev), (has_next, nxt)):
        @pl.when(there)
        def _(other=other):
            for f in (me, up, down):
                greet(other, f)

    loads = [pltpu.make_async_copy(an_ref, xb.at[3:6], lsem.at[0]), pltpu.make_async_copy(fn_ref, xb.at[0:3], lsem.at[1]),
             pltpu.make_async_copy(fo_ref, last.at[0:3], lsem.at[2]), pltpu.make_async_copy(ao_ref, last.at[3:6], lsem.at[3]),
             pltpu.make_async_copy(mod_ref, modr.at[me], lsem.at[4])]
    for copy in loads:
        copy.start()

    def onehot(shape, hit):
        a = lax.broadcasted_iota(jnp.int32, shape, 0)
        b = lax.broadcasted_iota(jnp.int32, shape, 1)
        return jnp.where(hit(a, b), 1.0, 0.0).astype(bf16)

    loads[0].wait()
    loads[1].wait()
    lane_id = lax.broadcasted_iota(jnp.int32, (rows, 128), 1)
    for way, source in enumerate((0, lanes - 128)):
        total = jnp.zeros((rows, 128), f32)
        for c in range(3):
            shift = (halo * c + (halo if way else 0)) % 128
            turned = xb[3 + c, :, source:source + 128]
            turned = pltpu.roll(turned, shift, 1) if shift else turned
            total = jnp.where((lane_id >= halo * c) & (lane_id < halo * (c + 1)), turned, total)
            if way == 0:
                turned = pltpu.roll(xb[c, :, :128], 3 * halo + 2 * c - 2, 1)
                spot = 3 * halo + 2 * c
                total = jnp.where((lane_id >= spot) & (lane_id < spot + 2), turned, total)
        stage[way, :rows] = total
        stage[way, rows:] = jnp.zeros((main - rows, 128), f32)

    pl.semaphore_wait(barrier, nf - 1 + 3 * (has_prev.astype(jnp.int32) + has_next.astype(jnp.int32)))

    @pl.when(has_prev)
    def _():
        for copy in to_prev:
            copy.start()
    for copy in to_ring + mod_send:
        copy.start()

    s_ref[...] = onehot((lanes, 2 * own), lambda a, b: (a % 2) * own + a // 2 == b)
    spot = lambda a: (a % 2) * 128 + (a // 128) * (2 * ORD) + (a % 128) // 2
    s1_ref[...] = onehot((256, 256), lambda a, b: (a % 128 < halo) & ((spot(a) == b) | (spot(a) + halo == b)))
    s2_ref[...] = onehot((256, 256), lambda a, b: (a % 128 < halo) & (spot(a) + 2 * halo == b))
    for l, (h, lo) in enumerate(tables):
        t3_ref[l, 0:halo] = h[own:]
        t3_ref[l, halo:2 * halo] = lo[own:]
        t3_ref[l, 2 * halo:3 * halo] = h[own:]
        t3_ref[l, 3 * halo:] = jnp.zeros((128 - 3 * halo, 2 * W), bf16)

    def samples(x, h_ref, l_ref):
        xh, xl = split(x)
        dh, dl = nn(xh, s_ref[...]).astype(bf16), nn(xl, s_ref[...]).astype(bf16)
        out = []
        for par in range(2):
            ph, plo = dh[:, par * own:(par + 1) * own], dl[:, par * own:(par + 1) * own]
            out.append(nn(ph, h_ref[:own]) + nn(ph, l_ref[:own]) + nn(plo, h_ref[:own]))
        return out

    for l, (h_ref, l_ref) in enumerate(tables):
        def ahead(c, carry, l=l, h_ref=h_ref, l_ref=l_ref):
            lc = 3 * l + c
            for par, out in enumerate(samples(xb[lc], h_ref, l_ref)):
                at = pl.ds(pl.multiple_of((2 * lc + par) * R, 8), rows)
                for b in range(2 * blocks):
                    uz[b, at, :] = out[:, 128 * b:128 * (b + 1)]
            return carry
        lax.fori_loop(0, 3, ahead, 0)

    @pl.when(has_next)
    def _():
        for copy in to_prev:
            copy.wait_recv()

    @pl.when(jnp.logical_not(has_next))
    def _():
        rh[...] = jnp.zeros_like(rh)
        ring[:, main:] = jnp.zeros((2, HR, 128), f32)
    for copy in to_ring:
        copy.wait_recv()
    for l, (h_ref, l_ref) in enumerate(tables):
        for par, out in enumerate(samples(rh[3 * l:3 * l + 3].reshape(3 * HR, lanes), h_ref, l_ref)):
            for c in range(3):
                at = (2 * (3 * l + c) + par) * R + main
                for b in range(2 * blocks):
                    uz[b, at:at + HR, :] = out[c * HR:(c + 1) * HR, 128 * b:128 * (b + 1)]
    for c in range(3):
        low, upper = ring[1], ring[0]
        if c:
            low, upper = pltpu.roll(low, 128 - halo * c, 1), pltpu.roll(upper, 128 - halo * c, 1)
        hh, hl = split(jnp.concatenate([low, upper], axis=1))
        he = (nn(hh, s1_ref[...]) + nn(hl, s2_ref[...])).astype(bf16)
        for par in range(2):
            at = (2 * (3 + c) + par) * R
            out = nn(he[:, par * 128:(par + 1) * 128], t3_ref[1])
            for b in range(2 * blocks):
                uz[b, at:at + R, :] += out[:, 128 * b:128 * (b + 1)]

    @pl.when(me == nf - 1)
    def _():
        for c in range(3):
            for par in range(2):
                spot = 3 * halo + 2 * c + par
                column = ring[0, :, spot:spot + 1]
                at = (2 * c + par) * R
                for b in range(blocks):
                    uz[b, at:at + R, :] += column * nyq_ref[0:1, 128 * b:128 * (b + 1)]

    loads[4].wait()
    for copy in mod_recv:
        copy.wait_recv()
    modx[...] = jnp.zeros_like(modx)
    for r in range(21):
        for d in range(nf):
            modx[r, :BASIS, 128 * d:128 * (d + 1)] = modr[d, r * BASIS:(r + 1) * BASIS, :] * wrow_ref[0:1, 128 * d:128 * (d + 1)]

    def moduli_step(t, carry):
        rows_two = []
        for k in range(2):
            h, lo = split(modx[2 * t + k])
            rows_two += [h, h, lo, jnp.zeros_like(h)]
        mt = nt(perm_ref[...], jnp.concatenate(rows_two, axis=0)).astype(bf16)
        for k in range(2):
            cs[pl.ds(pl.multiple_of((2 * t + k) * nodes, 8), nodes), :] = nn(mt[:, 128 * k:128 * (k + 1)], a3_ref[...])
        return carry

    lax.fori_loop(0, 11, moduli_step, 0)

    def point(a, j):
        p = wide * a + j
        return p % 2, p // 2 + (hrow if a == 4 * count_a else 0)

    def strain_step(t, carry):
        l, blk = t // blocks, t % blocks
        lane = pl.multiple_of(blk * 128, 128)
        blk_z = blocks + blk

        def grid(c, ea, at_blk):
            out = []
            for i in range(5):
                row = []
                for j in range(5):
                    par, r = point(4 * ea + i, j)
                    at = (2 * (3 * l + c) + par) * R + r
                    row.append(uz[at_blk, pl.ds(at, 8, stride=2), :])
                out.append(row)
            return out

        def put(v, ea, i, j, value):
            row = pl.multiple_of((6 * l + v) * nodes + ((ea * 5 + i) * 5 + j) * 8, 8)
            es[pl.ds(row, 8), pl.ds(lane, 128)] = value

        for ea in range(count_a):
            rad = lambda i, j: rad_ref[((ea * 5 + i) * 5 + j) * 8:((ea * 5 + i) * 5 + j) * 8 + 8, :]
            cols = lambda u: [[row[j] for row in u] for j in range(5)]
            u = grid(0, ea, blk)
            for j, col in enumerate(cols(u)):
                for i, v in enumerate(line(derive, col)):
                    put(0, ea, i, j, v)
            shear = [line(derive, row) for row in u]
            u = grid(1, ea, blk)
            for j, col in enumerate(cols(u)):
                for i, v in enumerate(line(derive, col)):
                    put(5, ea, i, j, v + shear[i][j])
            for i, row in enumerate(u):
                for j, v in enumerate(line(derive, row)):
                    put(1, ea, i, j, v)
            u = grid(2, ea, blk)
            z = grid(0, ea, blk_z)
            for j, col in enumerate(cols(u)):
                for i, v in enumerate(line(derive, col)):
                    put(4, ea, i, j, v + rad(i, j) * z[i][j])
            z = grid(1, ea, blk_z)
            for i, row in enumerate(u):
                for j, v in enumerate(line(derive, row)):
                    put(3, ea, i, j, v + rad(i, j) * z[i][j])
            z = grid(2, ea, blk_z)
            for i in range(5):
                for j in range(5):
                    put(2, ea, i, j, rad(i, j) * z[i][j])
        return carry

    lax.fori_loop(0, 2 * blocks, strain_step, 0)

    def node_step(t, carry):
        row = pl.multiple_of(t * 8, 8)
        at = lambda v: pl.ds(pl.multiple_of(v * nodes + row, 8), 8)

        def add(sums, v, term):
            sums[v] = term if sums[v] is None else sums[v] + term

        def one(ce, els):
            fw = [[es[at(v), el] for v in range(6)] for el in els]
            ad = [[es[at(6 + v), el] for v in range(6)] for el in els]
            sf = [[None] * 6 for _ in els]
            sa = [[None] * 6 for _ in els]
            for r, (v, w) in enumerate(PAIRS):
                c = cs[at(r), ce]
                total = None
                for f, a, tf, ta in zip(fw, ad, sf, sa):
                    add(tf, v, c * f[w])
                    add(ta, v, c * a[w])
                    if v != w:
                        add(tf, w, c * f[v])
                        add(ta, w, c * a[v])
                        prod = f[v] * a[w] + f[w] * a[v]
                    else:
                        prod = f[v] * a[v]
                    total = prod if total is None else total + prod
                ps[at(r), ce] = total
            for el, tf, ta in zip(els, sf, sa):
                for v in range(6):
                    es[at(v), el] = tf[v]
                    es[at(6 + v), el] = ta[v]

        for b in range(nb):
            one(slice(128 * b, 128 * b + 128),
                [slice(128 * b, 128 * b + 128), slice(128 * (nb + b), 128 * (nb + b) + 128)])
        one(slice(128 * nb, 128 * nb + 128), [slice(256 * nb, 256 * nb + 128)])
        return carry

    lax.fori_loop(0, nodes // 8, node_step, 0)

    def project_step(r, carry):
        ph, plo = split(ps[pl.ds(pl.multiple_of(r * nodes, 8), nodes), :])
        both = nt(aa_ref[...], ph)
        accb[r] = both[:32] + both[32:] + nt(aa_ref[:32], plo)
        return carry

    lax.fori_loop(0, 21, project_step, 0)
    h, lo = split(accb[...].reshape(21 * 32, nodes))
    whole = (nn(h, perm_ref[...]) + nn(lo, perm_ref[...])) * krow_ref[0:1, :]
    for d in range(nf):
        for r in range(21):
            kb[d, r * BASIS:(r + 1) * BASIS, :] = whole[32 * r:32 * r + BASIS, 128 * d:128 * (d + 1)]
        kb[d, 21 * BASIS:, :] = jnp.zeros((kb.shape[1] - 21 * BASIS, 128), f32)
    for copy in k_send:
        copy.start()

    def force_step(t, carry):
        l, blk = t // blocks, t % blocks
        lane = pl.multiple_of(blk * 128, 128)
        blk_z = blocks + blk
        top = lax.broadcasted_iota(jnp.int32, (8, 128), 0) == 0

        def get(v, ea, i, j):
            row = pl.multiple_of((6 * l + v) * nodes + ((ea * 5 + i) * 5 + j) * 8, 8)
            return es[pl.ds(row, 8), pl.ds(lane, 128)]

        def store(c, a, row, at_blk):
            def where(j):
                par, r = point(a, j)
                return (2 * (3 * l + c) + par) * R + r
            for j in range(1, 4):
                uz[at_blk, pl.ds(where(j), 8, stride=2), :] = row[j]
            back = pltpu.roll(row[4], 1, 0)
            uz[at_blk, pl.ds(where(0), 8, stride=2), :] = row[0] + jnp.where(top, 0.0, back)
            uz[at_blk, pl.ds(where(4) + 14, 1), :] = row[4][7:8]

        beyond = wide * (4 * count_a + 1)
        for c in range(3):
            held, held_z = None, None
            spare = (2 * (3 * l + c) + beyond % 2) * R + beyond // 2 + hrow
            for b in (blk, blk_z):
                uz[b, pl.ds(spare, 1), :] = jnp.zeros((1, 128), f32)
            for ea in range(count_a):
                rad = lambda i, j: rad_ref[((ea * 5 + i) * 5 + j) * 8:((ea * 5 + i) * 5 + j) * 8 + 8, :]
                cols = [line(derive.T, [get(PART_A[c], ea, i, j) for i in range(5)]) for j in range(5)]
                for i in range(5):
                    row = line(derive.T, [get(PART_B[c], ea, i, j) for j in range(5)])
                    row = [row[j] + cols[j][i] for j in range(5)]
                    row_z = [rad(i, j) * get(PART_P[c], ea, i, j) for j in range(5)]
                    if i == 0 and held is not None:
                        row = [p + q for p, q in zip(row, held)]
                        row_z = [p + q for p, q in zip(row_z, held_z)]
                    if i == 4 and ea + 1 < count_a:
                        held, held_z = row, row_z
                    else:
                        store(c, 4 * ea + i, row, blk)
                        store(c, 4 * ea + i, row_z, blk_z)
        return carry

    lax.fori_loop(0, 2 * blocks, force_step, 0)

    def interleave(values):
        h, lo = split(values)
        return nt(h, s_ref[...]) + nt(lo, s_ref[...])

    def turn_back(parts, l, with_edge):
        h_ref, l_ref = tables[1 - l]
        both, edge_h, edge_l = [], [], []
        for part in parts:
            h, lo = split(part)
            both.append(nt(h, h_ref[:own]) + nt(h, l_ref[:own]) + nt(lo, h_ref[:own]))
            if with_edge:
                edge_h.append(nt(h, t3_ref[1 - l]))
                edge_l.append(nt(lo, t3_ref[1 - l]))
        out = interleave(jnp.concatenate(both, axis=1))
        if not with_edge:
            return out, None
        h, lo = split(jnp.concatenate(edge_h, axis=1))
        side = nt(h, s1_ref[...]) + nt(lo, s1_ref[...])
        h, lo = split(jnp.concatenate(edge_l, axis=1))
        return out, side + nt(h, s2_ref[...]) + nt(lo, s2_ref[...])

    def spread(side, c):
        low, high = side[:, :128], side[:, 128:]
        return (pltpu.roll(low, halo * c, 1), pltpu.roll(high, halo * c, 1)) if c else (low, high)

    def read(lc, par, start, count):
        at = (2 * lc + par) * R + start
        return jnp.concatenate([uz[b, at:at + count, :] for b in range(2 * blocks)], axis=1)

    high = jnp.zeros((R, 128), f32)
    lane_r = lax.broadcasted_iota(jnp.int32, (R, 128), 1)
    for c in range(3):
        for par in range(2):
            at = (2 * (3 + c) + par) * R
            terms = None
            for b in range(blocks):
                term = uz[b, at:at + R, :] * nyq_ref[0:1, 128 * b:128 * (b + 1)]
                terms = term if terms is None else terms + term
            value = jnp.sum(terms, axis=1, keepdims=True) * is_last
            high = jnp.where(lane_r == 3 * halo + 2 * c + par, value, high)
    spill[0] = jnp.zeros((R, 128), f32)
    spill[1] = high

    for l in range(2):
        parts = [jnp.concatenate([read(3 * l + c, par, main, HR) for c in range(3)], axis=0) for par in range(2)]
        out, side = turn_back(parts, l, l == 0)
        edge_f[3 * l:3 * l + 3] = out.reshape(3, HR, lanes)
        if l == 0:
            for c in range(3):
                for way, value in enumerate(spread(side[c * HR:(c + 1) * HR], c)):
                    spill[way, main:] += value

    @pl.when(has_next)
    def _():
        for copy in to_next:
            copy.start()
    for c in range(3):
        out, side = turn_back([read(c, par, 0, main) for par in range(2)], 0, True)
        force[c] = out[:rows]
        for way, value in enumerate(spread(side, c)):
            spill[way, :main] += value
    for copy in to_spill:
        copy.start()
    for c in range(3):
        out, _ = turn_back([read(3 + c, par, 0, main) for par in range(2)], 1, False)
        force[3 + c] = out[:rows]

    lane_m = lax.broadcasted_iota(jnp.int32, (rows, 128), 1)

    def gather(start, count):
        for c in range(3):
            up_turned = rspill[1, start:start + count]
            up_turned = pltpu.roll(up_turned, 128 - halo * c, 1) if c else up_turned
            force[c, :count, :128] += jnp.where(lane_m[:count] < halo, up_turned, 0.0)
            low_turned = pltpu.roll(rspill[0, start:start + count], (128 - halo * (c + 1)), 1)
            force[c, :count, lanes - 128:] += jnp.where(lane_m[:count] >= 128 - halo, low_turned, 0.0)
            top_turned = pltpu.roll(rspill[1, start:start + count], 128 - 3 * halo - 2 * c + 2, 1)
            force[3 + c, :count, :128] += jnp.where((lane_m[:count] >= 2) & (lane_m[:count] < 4), top_turned, 0.0)

    @pl.when(has_prev)
    def _():
        for copy in to_next:
            copy.wait_recv()
        force[:, :edge] += rm[:, :edge]
        gather(main, edge)
    for copy in to_spill:
        copy.wait_recv()
    gather(0, rows)
    loads[2].wait()
    loads[3].wait()
    is_even = lax.broadcasted_iota(jnp.int32, (rows, lanes), 1) % 2 == 0
    mass = jnp.where(is_even, mass_ref[:, 0:1], mass_ref[:, 1:2])
    for c in range(3):
        f_ref[c] = 2.0 * xb[c] - last[c] - mass * force[c]
        a_ref[c] = 2.0 * xb[3 + c] - last[3 + c] - mass * force[3 + c]
    for copy in k_send:
        copy.wait_recv()
    total = kb[me]
    for s in range(nf - 1):
        total = total + kr[s]
    k_ref[...] = total

    @pl.when(has_prev)
    def _():
        for copy in to_prev:
            copy.wait_send()

    @pl.when(has_next)
    def _():
        for copy in to_next:
            copy.wait_send()
    for copy in to_ring + to_spill + mod_send + k_send:
        copy.wait_send()


def body(forward_now, forward_last, adjoint_now, adjoint_last, moduli, inv_radius, inv_mass):
    derive, weights = gll_tables()
    wide = 4 * EB + 1
    nf = lax.axis_size("fourier")
    nm = lax.axis_size("meridian")
    me = lax.axis_index("fourier")
    comps, rows, lanes = forward_now.shape
    local = lanes // 2
    total = local * nf
    orders = local // 2
    own = -(-local // 128) * 128
    row_count = 2 * rows // wide
    count_a = row_count // 4
    nodes_mine = moduli.shape[3]
    nodes = nodes_mine * nf
    edge = (wide + 1) // 2
    start = -(-rows // 8) * 8
    R = start + HR
    n, nb = sample_count(orders)
    W = 256 * nb + 128
    halo = 4 * ORD

    flat = jnp.pad(moduli[:, :, 0, :].reshape(21 * BASIS, nodes_mine),
                   ((0, -(21 * BASIS) % 8), (0, 128 - nodes_mine)))

    inner, first, last, halo_last = block_tables(orders, own)
    is_first = jnp.where(me == 0, 1.0, 0.0).astype(f32)
    is_last = jnp.where(me == nf - 1, 1.0, 0.0).astype(f32)
    head, tail = 24, slice(local - 2 * ORD, local)
    row = np.arange(own + halo)
    at_order = np.where(row < own, row // 2, np.where(row < own + 2 * ORD, (row - own) // 2 - ORD,
                                                      orders + (row - own - 2 * ORD) // 2))
    nyquist = (row // 2) == (own + 2 * ORD) // 2
    turn = jnp.asarray(at_order, f32) + (me * orders).astype(f32)
    turn = turn * (1.0 - jnp.asarray(nyquist, f32) * is_last)
    scale = jnp.concatenate([jnp.ones((own + halo, W), f32), jnp.broadcast_to(turn[:, None], (own + halo, W))], axis=1)
    fix_turned = with_turned(np.where(np.arange(head)[:, None] == 1, -inner[:head, :W], 0.0).astype(np.float32))
    parts_a = [inner[:head] + is_first * first[:head], inner[head:local - 2 * ORD] * jnp.ones((1, 1), f32),
               inner[tail] + is_last * last[tail], jnp.asarray(inner[local:own]),
               inner[own:] + is_first * first[own:] + is_last * last[own:]]
    parts_f = [inner[:head] + is_first * fix_turned, parts_a[1], jnp.asarray(inner[tail]), parts_a[3],
               is_last * halo_last[own:]]
    fh, fl = split_device(jnp.concatenate(parts_f, axis=0) * scale)
    ah, al = split_device(jnp.concatenate(parts_a, axis=0) * scale)

    rows_a = basis_rows(orders)
    bh, bl = split_host(rows_a)
    a3 = np.zeros((128, rows_a.shape[1]), bf16)
    a3[0:BASIS], a3[32:32 + BASIS], a3[64:64 + BASIS] = bh, bl, bh
    aa = np.zeros((64, rows_a.shape[1]), bf16)
    aa[0:BASIS], aa[32:32 + BASIS] = bh, bl
    perm = np.zeros((nodes, nf * 128), np.float32)
    wrow = np.zeros((8, nf * 128), np.float32)
    for ea in range(count_a):
        for eb in range(EB):
            for ij in range(25):
                q = (ea * EB + eb) * 25 + ij
                spot = (q // nodes_mine) * 128 + q % nodes_mine
                perm[(ea * 25 + ij) * EB + eb, spot] = 1.0
                wrow[:, spot] = weights[ij]
    radius = jnp.transpose(inv_radius.reshape(count_a, EB, 25), (0, 2, 1)).reshape(nodes, 1)
    radius = jnp.broadcast_to(radius, (nodes, 128))

    cfg = (nf, nm, own, R, wide, count_a, nodes, nb, start - rows, edge, derive)
    vmem = pl.BlockSpec(memory_space=pltpu.VMEM)
    hbm = pl.BlockSpec(memory_space=pl.ANY)
    CW = rows_a.shape[1]
    K_ROWS = flat.shape[0]
    copies = 11 + 2 * (nf - 1)
    field = jax.ShapeDtypeStruct((comps, rows, lanes), f32)
    forward_next, adjoint_next, sums = pl.pallas_call(
        functools.partial(core, cfg),
        out_shape=(field, field, jax.ShapeDtypeStruct((K_ROWS, 128), f32)),
        in_specs=[hbm] * 5 + [vmem] * 12,
        out_specs=(vmem, vmem, vmem),
        scratch_shapes=[pltpu.VMEM((2 * W // 128, 4 * comps * R, 128), f32), pltpu.VMEM((12 * nodes, W), f32),
                        pltpu.VMEM((22 * nodes, CW), f32), pltpu.VMEM((21 * nodes, CW), f32),
                        pltpu.VMEM((21, 32, nodes), f32), pltpu.VMEM((lanes, 2 * own), bf16),
                        pltpu.VMEM((256, 256), bf16), pltpu.VMEM((256, 256), bf16),
                        pltpu.VMEM((2, 128, 2 * W), bf16),
                        pltpu.VMEM((2 * comps, rows, lanes), f32), pltpu.VMEM((2 * comps, rows, lanes), f32),
                        pltpu.VMEM((nf, K_ROWS, 128), f32), pltpu.VMEM((22, 32, nf * 128), f32),
                        pltpu.VMEM((2 * comps, HR, lanes), f32), pltpu.VMEM((2, R - HR, 128), f32),
                        pltpu.VMEM((2, R, 128), f32), pltpu.VMEM((2 * comps, rows, lanes), f32),
                        pltpu.VMEM((2 * comps, HR, lanes), f32), pltpu.VMEM((2 * comps, HR, lanes), f32),
                        pltpu.VMEM((2, R, 128), f32), pltpu.VMEM((2, R, 128), f32),
                        pltpu.VMEM((nf, K_ROWS, 128), f32), pltpu.VMEM((nf - 1, K_ROWS, 128), f32),
                        pltpu.SemaphoreType.DMA((5,)), pltpu.SemaphoreType.DMA((copies,)),
                        pltpu.SemaphoreType.DMA((copies,))],
        compiler_params=pltpu.CompilerParams(vmem_limit_bytes=60 * 1024 * 1024, collective_id=0,
                                             has_side_effects=True),
    )(forward_now, forward_last, adjoint_now, adjoint_last, flat, radius, inv_mass.reshape(rows, 2), fh, fl, ah, al,
      jnp.asarray(perm.astype(bf16)), jnp.asarray(a3), jnp.asarray(aa), jnp.asarray(wrow * (2.0 / n)),
      jnp.asarray(wrow * (kernel_weight * 2.0 * total / n)),
      jnp.asarray(np.broadcast_to(0.5 * waves(orders)[0][orders + ORD], (8, W)).astype(np.float32)))
    sums = sums[:21 * BASIS, :nodes_mine].reshape(21, BASIS, 1, nodes_mine)
    return forward_next, adjoint_next, sums


def solution(mesh):
    field = P(None, "meridian", "fourier")
    grid = P(None, None, "meridian", "fourier")
    in_specs = (field, field, field, field, grid, P("meridian"), P("meridian"))
    return jax.shard_map(body, mesh=mesh, in_specs=in_specs, out_specs=(field, field, grid),
                         check_vma=False)
```

```python
import functools
import math

import jax
import jax.numpy as jnp
import numpy as np
from jax import lax
from jax.experimental import pallas as pl
from jax.experimental.pallas import tpu as pltpu
from jax.sharding import PartitionSpec as P

ORD = 8
EB = 8
BASIS = 2 * ORD + 1
HR = (4 * EB + 2) // 2 // 8 * 8 + 8
MESH = pl.DeviceIdType.MESH
kernel_weight = 0.0001
bf16 = jnp.bfloat16
f32 = jnp.float32
PAIRS = [(a, b) for a in range(6) for b in range(a, 6)]
PART_A, PART_B, PART_P = (0, 5, 4), (5, 1, 3), (4, 3, 2)


def gll_tables():
    x = np.array([-1.0, -math.sqrt(3.0 / 7.0), 0.0, math.sqrt(3.0 / 7.0), 1.0])
    weights = np.array([0.1, 49.0 / 90.0, 32.0 / 45.0, 49.0 / 90.0, 0.1])
    factor = np.array([np.prod([x[i] - x[k] for k in range(5) if k != i]) for i in range(5)])
    derive = np.zeros((5, 5))
    for i in range(5):
        for k in range(5):
            if i != k:
                derive[i, k] = factor[i] / (factor[k] * (x[i] - x[k]))
            else:
                derive[i, k] = sum(1.0 / (x[i] - x[o]) for o in range(5) if o != i)
    return derive, np.outer(weights, weights).reshape(25)


def sample_count(orders):
    n = orders + 2 * ORD + 1
    return n, 0 if n <= 64 else -(-(n - 64) // 128)


def place(re, im, nb):
    cut, n = 128 * nb, re.shape[1]
    rest = np.zeros((re.shape[0], 128))
    head = np.zeros((2, re.shape[0], cut))
    wide = min(n, cut)
    head[0, :, :wide], head[1, :, :wide] = re[:, :wide], im[:, :wide]
    if n > cut:
        rest[:, :n - cut], rest[:, 64:64 + n - cut] = re[:, cut:], im[:, cut:]
    return np.concatenate([head[0], head[1], rest], axis=1)


def waves(orders):
    n, nb = sample_count(orders)
    at = np.arange(-ORD, orders + ORD + 1)
    turn = 2 * np.pi * ((at[:, None] * np.arange(n)[None, :]) % n) / n
    return place(np.cos(turn), np.sin(turn), nb), place(np.sin(turn), -np.cos(turn), nb)


def with_turned(table):
    turned = np.zeros_like(table)
    turned[0::2], turned[1::2] = -table[1::2], table[0::2]
    return np.concatenate([table, turned], axis=1).astype(np.float32)


def block_tables(orders, own):
    ec, es = waves(orders)
    inner = np.zeros((own + 4 * ORD, ec.shape[1]))
    for row, p in [(2 * p, p) for p in range(orders)] + [(own + 2 * i, i - ORD) for i in range(ORD)] \
            + [(own + 2 * ORD + 2 * i, orders + i) for i in range(ORD)]:
        inner[row], inner[row + 1] = 0.5 * ec[p + ORD], 0.5 * es[p + ORD]
    first, last = np.zeros_like(inner), np.zeros_like(inner)
    first[0], first[1] = 0.5 * ec[ORD], -inner[1]
    for p in range(1, ORD + 1):
        first[2 * p] += 0.5 * ec[ORD - p]
        first[2 * p + 1] -= 0.5 * es[ORD - p]
    first[own:own + 2 * ORD] = -inner[own:own + 2 * ORD]
    last[own + 2 * ORD:] = -inner[own + 2 * ORD:]
    last[own + 2 * ORD + 1] += ec[orders + ORD]
    for j in range(1, ORD + 1):
        last[2 * (orders - j)] += 0.5 * ec[orders + j + ORD]
        last[2 * (orders - j) + 1] -= 0.5 * es[orders + j + ORD]
    halo_last = np.zeros_like(inner)
    halo_last[own + 2 * ORD + 1] = 0.5 * ec[orders + ORD]
    return [with_turned(t) for t in (inner, first, last, halo_last)]


def basis_rows(orders):
    n, nb = sample_count(orders)
    j = np.arange(BASIS)[:, None]
    turn = ((j + 1) // 2) * (2 * np.pi * np.arange(n)[None, :] / n)
    rows = np.where((j % 2 == 0) & (j > 0), np.sin(turn), np.cos(turn))
    both = place(rows, rows, nb)
    return both[:, 128 * nb:]


def split_host(values):
    wide = np.asarray(values, np.float32)
    hi = wide.astype(bf16)
    return hi, (wide - hi.astype(np.float32)).astype(bf16)


def split_device(values):
    hi = lax.reduce_precision(values, 8, 7)
    return hi.astype(bf16), (values - hi).astype(bf16)


def split(values):
    hi = values.astype(bf16)
    return hi, (values - hi.astype(f32)).astype(bf16)


def nt(a, b):
    return lax.dot_general(a, b, (((1,), (1,)), ((), ())), preferred_element_type=f32)


def nn(a, b):
    return lax.dot_general(a, b, (((1,), (0,)), ((), ())), preferred_element_type=f32)


def line(matrix, u):
    s0, d0, s1, d1 = u[0] + u[4], u[0] - u[4], u[1] + u[3], u[1] - u[3]
    out = [None] * 5
    for i in range(2):
        m = [float(v) for v in matrix[i]]
        odd = (0.5 * (m[0] - m[4])) * d0 + (0.5 * (m[1] - m[3])) * d1
        even = (0.5 * (m[0] + m[4])) * s0 + (0.5 * (m[1] + m[3])) * s1 + m[2] * u[2]
        out[i], out[4 - i] = even + odd, odd - even
    m = [float(v) for v in matrix[2]]
    out[2] = m[0] * d0 + m[1] * d1
    return out


def core(cfg, fn_ref, fo_ref, an_ref, ao_ref, mod_ref, inner_ref, fix_ref, perm_in, rrow_ref, mrow_ref,
         a3_ref, aa_ref, wrow_ref, krow_ref, nyq_ref, f_ref, a_ref, k_ref,
         uz, es, cs, ps, accb, s_ref, s1_ref, s2_ref, t3_ref, xb, last, modr, modx, rh, stage, ring, force,
         edge_f, rm, spill, rspill, kb, kr, ks, rad_ref, mass_ref, tab_h, tab_l, inner_v, fix_v, perm_ref,
         pack, rpack, edge_p, rmp, x3, lsem, ssem, rsem):
    nf, nm, own, R, wide, count_a, nodes, nb, hrow, edge, own_orders, derive = cfg
    rows, lanes = fn_ref.shape[1:]
    W = 256 * nb + 128
    blocks = 2 * nb + 1
    halo = 4 * ORD
    main = R - HR
    tables = tuple((tab_h.at[l], tab_l.at[l]) for l in range(2))
    orders = own_orders
    me, mi = lax.axis_index("fourier"), lax.axis_index("meridian")
    up, down = lax.rem(me + 1, nf), lax.rem(me + nf - 1, nf)
    has_prev, has_next = mi > 0, mi < nm - 1
    is_last = jnp.where(me == nf - 1, 1.0, 0.0).astype(f32)

    def remote(src, dst, at, meridian, fourier):
        return pltpu.make_async_remote_copy(
            src_ref=src, dst_ref=dst, send_sem=ssem.at[at], recv_sem=rsem.at[at],
            device_id={"meridian": meridian, "fourier": fourier}, device_id_type=MESH)

    half = nf // 2
    odd = lax.rem(me, 2)
    partner, mine = me + 1 - 2 * odd, me // 2
    peers = [2 * lax.rem(mine + s + 1, half) + odd for s in range(half - 1)]
    sources = [2 * lax.rem(mine + half - 1 - s, half) + odd for s in range(half - 1)]
    first, top = pl.ds(0, HR), pl.ds(0, edge - 1)
    body_rows, tail_rows = pl.ds(0, main), pl.ds(main, HR)
    prev, nxt = mi - 1, mi + 1
    to_prev = [remote(fn_ref.at[:, top], rh.at[0:3], 0, prev, me),
               remote(an_ref.at[:, top], rh.at[3:6], 1, prev, me),
               remote(pack, rpack, 2, prev, me),
               remote(stage.at[0, first], ring.at[0, tail_rows], 3, prev, down),
               remote(stage.at[1, first], ring.at[1, tail_rows], 4, prev, up)]
    to_ring = [remote(stage.at[0], ring.at[0, body_rows], 5, mi, down),
               remote(stage.at[1], ring.at[1, body_rows], 6, mi, up)]
    to_next = [remote(edge_f, rm, 7, nxt, me), remote(edge_p, rmp, 8, nxt, me),
               remote(spill.at[0, tail_rows], rspill.at[0, tail_rows], 9, nxt, down),
               remote(spill.at[1, tail_rows], rspill.at[1, tail_rows], 10, nxt, up)]
    to_spill = [remote(spill.at[0, body_rows], rspill.at[0, body_rows], 11, mi, down),
                remote(spill.at[1, body_rows], rspill.at[1, body_rows], 12, mi, up)]
    base = 13
    mod_far = [remote(mod_ref, modr.at[me], base + s, mi, peers[s]) for s in range(half - 1)]
    mod_got = [remote(mod_ref, modr.at[sources[s]], base + s, mi, peers[s]) for s in range(half - 1)]
    base += half - 1
    mod_near = remote(mod_ref, modr.at[me], base, mi, partner)
    near_got = remote(mod_ref, modr.at[partner], base, mi, partner)
    mod_pass = [remote(modr.at[sources[s]], modr.at[sources[s]], base + 1 + s, mi, partner) for s in range(half - 1)]
    pass_got = [remote(modr.at[sources[s]], modr.at[sources[s] + 1 - 2 * odd], base + 1 + s, mi, partner)
                for s in range(half - 1)]
    base += half
    k_near = remote(kb.at[1 - odd], kr, base, mi, partner)
    k_far = [remote(kb.at[odd, lax.rem(mine + s + 1, half)], ks.at[s], base + 1 + s, mi, peers[s])
             for s in range(half - 1)]

    barrier = pltpu.get_barrier_semaphore()

    def greet(meridian, fourier):
        pl.semaphore_signal(barrier, inc=1, device_id={"meridian": meridian, "fourier": fourier},
                            device_id_type=MESH)

    for s in range(1, nf):
        greet(mi, lax.rem(me + s, nf))
    for there, other in ((has_prev, prev), (has_next, nxt)):
        @pl.when(there)
        def _(other=other):
            for f in (me, up, down):
                greet(other, f)

    loads = [pltpu.make_async_copy(an_ref, xb.at[3:6], lsem.at[0]), pltpu.make_async_copy(fn_ref, xb.at[0:3], lsem.at[1]),
             pltpu.make_async_copy(fo_ref, last.at[0:3], lsem.at[2]), pltpu.make_async_copy(ao_ref, last.at[3:6], lsem.at[3]),
             pltpu.make_async_copy(mod_ref, modr.at[me], lsem.at[4]),
             pltpu.make_async_copy(inner_ref, inner_v, lsem.at[5]), pltpu.make_async_copy(fix_ref, fix_v, lsem.at[6]),
             pltpu.make_async_copy(perm_in, perm_ref, lsem.at[7])]
    for copy in loads:
        copy.start()

    def onehot(shape, hit):
        a = lax.broadcasted_iota(jnp.int32, shape, 0)
        b = lax.broadcasted_iota(jnp.int32, shape, 1)
        return jnp.where(hit(a, b), 1.0, 0.0).astype(bf16)

    loads[0].wait()
    loads[1].wait()
    lane_id = lax.broadcasted_iota(jnp.int32, (rows, 128), 1)
    for way, source in enumerate((0, lanes - 128)):
        total = jnp.zeros((rows, 128), f32)
        for c in range(3):
            shift = (halo * c + (halo if way else 0)) % 128
            turned = xb[3 + c, :rows, source:source + 128]
            turned = pltpu.roll(turned, shift, 1) if shift else turned
            total = jnp.where((lane_id >= halo * c) & (lane_id < halo * (c + 1)), turned, total)
            if way == 0:
                turned = pltpu.roll(xb[c, :rows, :128], 3 * halo + 2 * c - 2, 1)
                spot = 3 * halo + 2 * c
                total = jnp.where((lane_id >= spot) & (lane_id < spot + 2), turned, total)
        stage[way, :rows] = total
        stage[way, rows:] = jnp.zeros((main - rows, 128), f32)

    for lc in range(6):
        pack[lc:lc + 1, :] = xb[lc, edge - 1:edge, :]
    pack[6:, :] = jnp.zeros((2, lanes), f32)
    pl.semaphore_wait(barrier, nf - 1 + 3 * (has_prev.astype(jnp.int32) + has_next.astype(jnp.int32)))

    @pl.when(has_prev)
    def _():
        for copy in to_prev:
            copy.start()
    for copy in to_ring + mod_far + [mod_near]:
        copy.start()

    lane8 = lax.broadcasted_iota(jnp.int32, (8, 128), 1)
    sub8 = lax.broadcasted_iota(jnp.int32, (8, 128), 0)

    def column(row_ref, lowest, highest, index):
        total = jnp.zeros((8, 128), f32)
        for b in range(lowest // 128, highest // 128 + 1):
            width = min(128, row_ref.shape[1] - 128 * b)
            values = jnp.broadcast_to(row_ref[0:1, 128 * b:128 * b + width], (8, width))
            if width < 128:
                values = jnp.concatenate([values, jnp.zeros((8, 128 - width), f32)], axis=1)
            total = total + jnp.where(lane8 + 128 * b == index, values, 0.0)
        return jnp.broadcast_to(jnp.sum(total, axis=1, keepdims=True), (8, 128))

    per_row = nodes // count_a
    for ea in range(count_a):
        for ij in range(25):
            at = (ea * 25 + ij) * 8
            rad_ref[at:at + 8, :] = column(rrow_ref, ea * per_row + ij, ea * per_row + ij + 25 * (EB - 1),
                                           25 * sub8 + (ea * per_row + ij))
    for i in range(-(-rows // 8)):
        high = min(16 * i + 15, mrow_ref.shape[1] - 1)
        mass_0 = column(mrow_ref, 16 * i, high, 2 * sub8 + 16 * i)
        mass_1 = column(mrow_ref, 16 * i, high, 2 * sub8 + (16 * i + 1))
        mass_ref[8 * i:8 * i + 8, :] = jnp.where(lane8 % 2 == 0, mass_0, mass_1)
    loads[5].wait()
    loads[6].wait()
    is_first = jnp.where(me == 0, 1.0, 0.0).astype(f32)
    sub16 = lax.broadcasted_iota(jnp.int32, (16, W), 0)
    start_order = (me * orders).astype(f32)

    def put_rows(ls, at, value, turn):
        h, lo = split(jnp.concatenate([value[:, :W], value[:, W:] * turn], axis=1))
        for l in ls:
            tab_h[l, pl.ds(at, 16)] = h
            tab_l[l, pl.ds(at, 16)] = lo

    def table_step(g, carry):
        at = pl.multiple_of(g * 16, 16)
        put_rows((0, 1), at, inner_v[pl.ds(at, 16), :], (8 * g + sub16 // 2).astype(f32) + start_order)
        return carry

    lax.fori_loop(0, own // 16, table_step, 0)
    for g in range(2):
        at, turn = 16 * g, (8 * g + sub16 // 2).astype(f32) + start_order
        put_rows((1,), at, inner_v[at:at + 16] + is_first * fix_v[at:at + 16], turn)
        put_rows((0,), at, inner_v[at:at + 16] + is_first * fix_v[32 + at:48 + at], turn)
        at, low = own + 16 * g, (orders if g else -ORD)
        turn = (low + sub16 // 2).astype(f32) + start_order
        if g:
            turn = jnp.where(sub16 < 2, turn * (1.0 - is_last), turn)
        put_rows((1,), at, inner_v[at:at + 16] + is_first * fix_v[80 + 16 * g:96 + 16 * g]
                 + is_last * fix_v[112 + 16 * g:128 + 16 * g], turn)
        put_rows((0,), at, is_last * fix_v[144 + 16 * g:160 + 16 * g], turn)
    at = 2 * orders - 16
    put_rows((1,), at, inner_v[at:at + 16] + is_last * fix_v[64:80],
             (at // 2 + sub16 // 2).astype(f32) + start_order)

    s_ref[...] = onehot(s_ref.shape, lambda a, b: (a % 2) * 128 + a // 2 == b)
    spot = lambda a: (a % 2) * 128 + (a // 128) * (2 * ORD) + (a % 128) // 2
    s1_ref[...] = onehot((256, 256), lambda a, b: (a % 128 < halo) & ((spot(a) == b) | (spot(a) + halo == b)))
    s2_ref[...] = onehot((256, 256), lambda a, b: (a % 128 < halo) & (spot(a) + 2 * halo == b))
    for l, (h, lo) in enumerate(tables):
        t3_ref[l, 0:halo] = h[own:]
        t3_ref[l, halo:2 * halo] = lo[own:]
        t3_ref[l, 2 * halo:3 * halo] = h[own:]
        t3_ref[l, 3 * halo:] = jnp.zeros((128 - 3 * halo, 2 * W), bf16)

    lane_blocks = own // 128
    bw = lanes // lane_blocks

    def apart(x):
        out = [nn(x[:, bw * b:bw * (b + 1)], s_ref[...]).astype(bf16) for b in range(lane_blocks)]
        return [jnp.concatenate([o[:, 128 * par:128 * (par + 1)] for o in out], axis=1) for par in range(2)]

    def samples(x, h_ref, l_ref, keep):
        xh, xl = split(x)
        hi, lo = apart(xh), apart(xl)
        for n in range(2 * W // 256):
            ln = slice(256 * n, 256 * (n + 1))
            for par in range(2):
                keep(par, n, nn(hi[par], h_ref[:own, ln]) + nn(hi[par], l_ref[:own, ln]) + nn(lo[par], h_ref[:own, ln]))

    def ahead(l, carry):
        def keep(par, n, out):
            for c in range(3):
                at = pl.ds(pl.multiple_of((2 * (3 * l + c) + par) * R, 8), main)
                for k in range(2):
                    uz[2 * n + k, at, :] = out[c * main:(c + 1) * main, 128 * k:128 * (k + 1)]
        for c in range(3):
            x3[c * main:c * main + rows, :] = xb[3 * l + c]
        samples(x3[...], tab_h.at[l], tab_l.at[l], keep)
        return carry

    lax.fori_loop(0, 2, ahead, 0)

    @pl.when(has_next)
    def _():
        for copy in to_prev:
            copy.wait_recv()

    @pl.when(jnp.logical_not(has_next))
    def _():
        rh[...] = jnp.zeros_like(rh)
        rpack[...] = jnp.zeros_like(rpack)
        ring[:, main:] = jnp.zeros((2, HR, 128), f32)
    for copy in to_ring:
        copy.wait_recv()
    for copy, forward in zip(mod_got, mod_pass):
        copy.wait_recv()
        forward.start()
    count = edge - 1
    for l, (h_ref, l_ref) in enumerate(tables):
        def keep(par, n, out, l=l):
            for c in range(3):
                at = (2 * (3 * l + c) + par) * R + main
                for k in range(2):
                    ln = slice(128 * k, 128 * (k + 1))
                    uz[2 * n + k, at:at + count, :] = out[c * count:(c + 1) * count, ln]
                    uz[2 * n + k, at + count:at + edge, :] = out[3 * count + 3 * l + c:3 * count + 3 * l + c + 1, ln]
        x = jnp.concatenate([rh[3 * l:3 * l + 3].reshape(3 * count, lanes), rpack[...]], axis=0)
        samples(x, h_ref, l_ref, keep)
    for c in range(3):
        low, upper = ring[1], ring[0]
        if c:
            low, upper = pltpu.roll(low, 128 - halo * c, 1), pltpu.roll(upper, 128 - halo * c, 1)
        hh, hl = split(jnp.concatenate([low, upper], axis=1))
        he = (nn(hh, s1_ref[...]) + nn(hl, s2_ref[...])).astype(bf16)
        for par in range(2):
            at = (2 * (3 + c) + par) * R
            out = nn(he[:, par * 128:(par + 1) * 128], t3_ref[1])
            for b in range(2 * blocks):
                uz[b, at:at + R, :] += out[:, 128 * b:128 * (b + 1)]

    @pl.when(me == nf - 1)
    def _():
        for c in range(3):
            for par in range(2):
                spot = 3 * halo + 2 * c + par
                column = ring[0, :, spot:spot + 1]
                at = (2 * c + par) * R
                for b in range(blocks):
                    uz[b, at:at + R, :] += column * nyq_ref[0:1, 128 * b:128 * (b + 1)]

    loads[4].wait()
    near_got.wait_recv()
    for copy in pass_got:
        copy.wait_recv()
    loads[7].wait()
    modx[...] = jnp.zeros_like(modx)
    for r in range(21):
        for d in range(nf):
            ln = slice(128 * d, 128 * d + modr.shape[2])
            modx[r, :BASIS, ln] = modr[d, r * BASIS:(r + 1) * BASIS, :] * wrow_ref[0:1, ln]

    row_nodes, row_lanes = nodes // count_a, nf * 128 // count_a
    pairs_each = -(-11 // (2 * blocks))

    def moduli_pair(t):
        rows_two = []
        for k in range(2):
            h, lo = split(modx[2 * t + k])
            rows_two += [h, h, lo, jnp.zeros_like(h)]
        two = jnp.concatenate(rows_two, axis=0)
        for ea in range(count_a):
            ln = slice(ea * row_lanes, (ea + 1) * row_lanes)
            mt = nt(perm_ref[ea * row_nodes:(ea + 1) * row_nodes, ln], two[:, ln]).astype(bf16)
            for k in range(2):
                at = pl.multiple_of((2 * t + k) * nodes + ea * row_nodes, 8)
                cs[pl.ds(at, row_nodes), :] = nn(mt[:, 128 * k:128 * (k + 1)], a3_ref[...])

    def point(a, j):
        p = wide * a + j
        return p % 2, p // 2 + (hrow if a == 4 * count_a else 0)

    def strain_step(t, carry):
        l, blk = t // blocks, t % blocks
        lane = pl.multiple_of(blk * 128, 128)
        blk_z = blocks + blk

        def grid(c, ea, at_blk):
            out = []
            for i in range(5):
                row = []
                for j in range(5):
                    par, r = point(4 * ea + i, j)
                    at = (2 * (3 * l + c) + par) * R + r
                    row.append(uz[at_blk, pl.ds(at, 8, stride=2), :])
                out.append(row)
            return out

        def put(v, ea, i, j, value):
            row = pl.multiple_of((6 * l + v) * nodes + ((ea * 5 + i) * 5 + j) * 8, 8)
            es[pl.ds(row, 8), pl.ds(lane, 128)] = value

        for ea in range(count_a):
            rad = lambda i, j: rad_ref[((ea * 5 + i) * 5 + j) * 8:((ea * 5 + i) * 5 + j) * 8 + 8, :]
            cols = lambda u: [[row[j] for row in u] for j in range(5)]
            u = grid(0, ea, blk)
            for j, col in enumerate(cols(u)):
                for i, v in enumerate(line(derive, col)):
                    put(0, ea, i, j, v)
            shear = [line(derive, row) for row in u]
            u = grid(1, ea, blk)
            for j, col in enumerate(cols(u)):
                for i, v in enumerate(line(derive, col)):
                    put(5, ea, i, j, v + shear[i][j])
            for i, row in enumerate(u):
                for j, v in enumerate(line(derive, row)):
                    put(1, ea, i, j, v)
            u = grid(2, ea, blk)
            z = grid(0, ea, blk_z)
            for j, col in enumerate(cols(u)):
                for i, v in enumerate(line(derive, col)):
                    put(4, ea, i, j, v + rad(i, j) * z[i][j])
            z = grid(1, ea, blk_z)
            for i, row in enumerate(u):
                for j, v in enumerate(line(derive, row)):
                    put(3, ea, i, j, v + rad(i, j) * z[i][j])
            z = grid(2, ea, blk_z)
            for i in range(5):
                for j in range(5):
                    put(2, ea, i, j, rad(i, j) * z[i][j])
        for k in range(pairs_each):
            moduli_pair(t * pairs_each + k)
        return carry

    lax.fori_loop(0, 2 * blocks, strain_step, 0)

    def node_step(t, carry):
        row = pl.multiple_of(t * 8, 8)
        at = lambda v: pl.ds(pl.multiple_of(v * nodes + row, 8), 8)

        def add(sums, v, term):
            sums[v] = term if sums[v] is None else sums[v] + term

        def one(ce, els):
            fw = [[es[at(v), el] for v in range(6)] for el in els]
            ad = [[es[at(6 + v), el] for v in range(6)] for el in els]
            sf = [[None] * 6 for _ in els]
            sa = [[None] * 6 for _ in els]
            for r, (v, w) in enumerate(PAIRS):
                c = cs[at(r), ce]
                total = None
                for f, a, tf, ta in zip(fw, ad, sf, sa):
                    add(tf, v, c * f[w])
                    add(ta, v, c * a[w])
                    if v != w:
                        add(tf, w, c * f[v])
                        add(ta, w, c * a[v])
                        prod = f[v] * a[w] + f[w] * a[v]
                    else:
                        prod = f[v] * a[v]
                    total = prod if total is None else total + prod
                ps[at(r), ce] = total
            for el, tf, ta in zip(els, sf, sa):
                for v in range(6):
                    es[at(v), el] = tf[v]
                    es[at(6 + v), el] = ta[v]

        for b in range(nb):
            one(slice(128 * b, 128 * b + 128),
                [slice(128 * b, 128 * b + 128), slice(128 * (nb + b), 128 * (nb + b) + 128)])
        one(slice(128 * nb, 128 * nb + 128), [slice(256 * nb, 256 * nb + 128)])
        return carry

    lax.fori_loop(0, nodes // 8, node_step, 0)

    each = -(-21 // (2 * blocks))

    def project(r):
        ph, plo = split(ps[pl.ds(pl.multiple_of(r * nodes, 8), nodes), :])
        both = nt(aa_ref[...], ph)
        accb[r] = both[:32] + both[32:] + nt(aa_ref[:32], plo)

    def force_step(t, carry):
        l, blk = t // blocks, t % blocks
        lane = pl.multiple_of(blk * 128, 128)
        blk_z = blocks + blk
        top = lax.broadcasted_iota(jnp.int32, (8, 128), 0) == 0

        def get(v, ea, i, j):
            row = pl.multiple_of((6 * l + v) * nodes + ((ea * 5 + i) * 5 + j) * 8, 8)
            return es[pl.ds(row, 8), pl.ds(lane, 128)]

        def store(c, a, row, at_blk):
            def where(j):
                par, r = point(a, j)
                return (2 * (3 * l + c) + par) * R + r
            for j in range(1, 4):
                uz[at_blk, pl.ds(where(j), 8, stride=2), :] = row[j]
            back = pltpu.roll(row[4], 1, 0)
            uz[at_blk, pl.ds(where(0), 8, stride=2), :] = row[0] + jnp.where(top, 0.0, back)
            uz[at_blk, pl.ds(where(4) + 14, 1), :] = row[4][7:8]

        beyond = wide * (4 * count_a + 1)
        for c in range(3):
            held, held_z = None, None
            spare = (2 * (3 * l + c) + beyond % 2) * R + beyond // 2 + hrow
            for b in (blk, blk_z):
                uz[b, pl.ds(spare, 1), :] = jnp.zeros((1, 128), f32)
            for ea in range(count_a):
                rad = lambda i, j: rad_ref[((ea * 5 + i) * 5 + j) * 8:((ea * 5 + i) * 5 + j) * 8 + 8, :]
                cols = [line(derive.T, [get(PART_A[c], ea, i, j) for i in range(5)]) for j in range(5)]
                for i in range(5):
                    row = line(derive.T, [get(PART_B[c], ea, i, j) for j in range(5)])
                    row = [row[j] + cols[j][i] for j in range(5)]
                    row_z = [rad(i, j) * get(PART_P[c], ea, i, j) for j in range(5)]
                    if i == 0 and held is not None:
                        row = [p + q for p, q in zip(row, held)]
                        row_z = [p + q for p, q in zip(row_z, held_z)]
                    if i == 4 and ea + 1 < count_a:
                        held, held_z = row, row_z
                    else:
                        store(c, 4 * ea + i, row, blk)
                        store(c, 4 * ea + i, row_z, blk_z)
        for k in range(each):
            project(t * each + k)
        return carry

    lax.fori_loop(0, 2 * blocks, force_step, 0)
    h, lo = split(accb[:21].reshape(21 * 32, nodes))
    for ea in range(count_a):
        q, ln = slice(ea * row_nodes, (ea + 1) * row_nodes), slice(ea * row_lanes, (ea + 1) * row_lanes)
        part = (nn(h[:, q], perm_ref[q, ln]) + nn(lo[:, q], perm_ref[q, ln])) * krow_ref[0:1, ln]
        for k in range(nf // count_a):
            for r in range(21):
                d = ea * (nf // count_a) + k
                kb[d % 2, d // 2, r * BASIS:(r + 1) * BASIS, :] = \
                    part[32 * r:32 * r + BASIS, 128 * k:128 * k + kb.shape[3]]
    k_near.start()

    def interleave(both):
        out = []
        for b in range(lane_blocks):
            ln = slice(128 * b, 128 * (b + 1))
            h, lo = split(jnp.concatenate([both[0][:, ln], both[1][:, ln]], axis=1))
            out.append(nt(h, s_ref[...]) + nt(lo, s_ref[...]))
        return jnp.concatenate(out, axis=1)

    def turn_back(parts, l, with_edge):
        h_ref, l_ref = tables[1 - l]
        both, edge_h, edge_l = [], [], []
        for part in parts:
            h, lo = split(part)
            both.append(nt(h, h_ref[:own]) + nt(h, l_ref[:own]) + nt(lo, h_ref[:own]))
            if with_edge:
                edge_h.append(nt(h, t3_ref[1 - l]))
                edge_l.append(nt(lo, t3_ref[1 - l]))
        out = interleave(both)
        if not with_edge:
            return out, None
        h, lo = split(jnp.concatenate(edge_h, axis=1))
        side = nt(h, s1_ref[...]) + nt(lo, s1_ref[...])
        h, lo = split(jnp.concatenate(edge_l, axis=1))
        return out, side + nt(h, s2_ref[...]) + nt(lo, s2_ref[...])

    def spread(side, c):
        low, high = side[:, :128], side[:, 128:]
        return (pltpu.roll(low, halo * c, 1), pltpu.roll(high, halo * c, 1)) if c else (low, high)

    def read(lc, par, start, count):
        at = (2 * lc + par) * R + start
        return jnp.concatenate([uz[b, at:at + count, :] for b in range(2 * blocks)], axis=1)

    high = jnp.zeros((R, 128), f32)
    lane_r = lax.broadcasted_iota(jnp.int32, (R, 128), 1)
    for c in range(3):
        for par in range(2):
            at = (2 * (3 + c) + par) * R
            terms = None
            for b in range(blocks):
                term = uz[b, at:at + R, :] * nyq_ref[0:1, 128 * b:128 * (b + 1)]
                terms = term if terms is None else terms + term
            value = jnp.sum(terms, axis=1, keepdims=True) * is_last
            high = jnp.where(lane_r == 3 * halo + 2 * c + par, value, high)
    spill[0] = jnp.zeros((R, 128), f32)
    spill[1] = high

    for l in range(2):
        parts = [jnp.concatenate([read(3 * l + c, par, main, HR) for c in range(3)], axis=0) for par in range(2)]
        out, side = turn_back(parts, l, l == 0)
        for c in range(3):
            edge_f[3 * l + c] = out[c * HR:c * HR + count]
            edge_p[3 * l + c:3 * l + c + 1, :] = out[c * HR + count:c * HR + edge]
        if l == 0:
            for c in range(3):
                for way, value in enumerate(spread(side[c * HR:(c + 1) * HR], c)):
                    spill[way, main:] += value

    edge_p[6:, :] = jnp.zeros((2, lanes), f32)

    @pl.when(has_next)
    def _():
        for copy in to_next:
            copy.start()
    k_near.wait_recv()
    k_near.wait_send()
    kb[odd] += kr[...]
    for copy in k_far:
        copy.start()
    for c in range(3):
        out, side = turn_back([read(c, par, 0, main) for par in range(2)], 0, True)
        force[c] = out[:rows]
        for way, value in enumerate(spread(side, c)):
            spill[way, :main] += value
    for copy in to_spill:
        copy.start()

    def adjoint_back(c, carry):
        at = [pl.ds(pl.multiple_of((2 * (3 + c) + par) * R, 8), main) for par in range(2)]
        parts = [jnp.concatenate([uz[b, a, :] for b in range(2 * blocks)], axis=1) for a in at]
        out, _ = turn_back(parts, 1, False)
        force[3 + c] = out[:rows]
        return carry

    lax.fori_loop(0, 3, adjoint_back, 0)

    lane_m = lax.broadcasted_iota(jnp.int32, (rows, 128), 1)

    def gather(start, count):
        for c in range(3):
            up_turned = rspill[1, start:start + count]
            up_turned = pltpu.roll(up_turned, 128 - halo * c, 1) if c else up_turned
            force[c, :count, :128] += jnp.where(lane_m[:count] < halo, up_turned, 0.0)
            low_turned = pltpu.roll(rspill[0, start:start + count], (128 - halo * (c + 1)), 1)
            force[c, :count, lanes - 128:] += jnp.where(lane_m[:count] >= 128 - halo, low_turned, 0.0)
            top_turned = pltpu.roll(rspill[1, start:start + count], 128 - 3 * halo - 2 * c + 2, 1)
            force[3 + c, :count, :128] += jnp.where((lane_m[:count] >= 2) & (lane_m[:count] < 4), top_turned, 0.0)

    @pl.when(has_prev)
    def _():
        for copy in to_next:
            copy.wait_recv()
        force[:, :edge - 1] += rm[...]
        for lc in range(6):
            force[lc, edge - 1:edge, :] += rmp[lc:lc + 1, :]
        gather(main, edge)
    for copy in to_spill:
        copy.wait_recv()
    gather(0, rows)
    loads[2].wait()
    loads[3].wait()
    mass = jnp.concatenate([mass_ref[:rows]] * (lanes // 128), axis=1)
    for c in range(3):
        f_ref[c] = 2.0 * xb[c, :rows] - last[c] - mass * force[c]
        a_ref[c] = 2.0 * xb[3 + c, :rows] - last[3 + c] - mass * force[3 + c]
    for copy in k_far:
        copy.wait_recv()
    total = kb[odd, mine]
    for s in range(half - 1):
        total = total + ks[s]
    for r in range(21):
        k_ref[r, :, 0, :] = total[r * BASIS:(r + 1) * BASIS]

    @pl.when(has_prev)
    def _():
        for copy in to_prev:
            copy.wait_send()

    @pl.when(has_next)
    def _():
        for copy in to_next:
            copy.wait_send()
    for copy in to_ring + to_spill + mod_far + [mod_near] + mod_pass + k_far:
        copy.wait_send()


def body(forward_now, forward_last, adjoint_now, adjoint_last, moduli, inv_radius, inv_mass):
    derive, weights = gll_tables()
    wide = 4 * EB + 1
    nf = lax.axis_size("fourier")
    nm = lax.axis_size("meridian")
    me = lax.axis_index("fourier")
    comps, rows, lanes = forward_now.shape
    local = lanes // 2
    total = local * nf
    orders = local // 2
    own = -(-local // 128) * 128
    row_count = 2 * rows // wide
    count_a = row_count // 4
    nodes_mine = moduli.shape[3]
    nodes = nodes_mine * nf
    edge = (wide + 1) // 2
    start = -(-rows // 8) * 8
    R = start + HR
    n, nb = sample_count(orders)
    W = 256 * nb + 128
    halo = 4 * ORD

    flat = moduli.reshape(21 * BASIS, nodes_mine)

    inner, first, last, halo_last = block_tables(orders, own)
    drop = np.zeros_like(first[:32])
    drop[:] = with_turned(np.where(np.arange(32)[:, None] == 1, -inner[:32, :W], 0.0))
    fixes = np.concatenate([first[:32], drop, last[local - 16:local], first[own:], last[own:], halo_last[own:]], axis=0)

    rows_a = basis_rows(orders)
    bh, bl = split_host(rows_a)
    a3 = np.zeros((128, rows_a.shape[1]), bf16)
    a3[0:BASIS], a3[32:32 + BASIS], a3[64:64 + BASIS] = bh, bl, bh
    aa = np.zeros((64, rows_a.shape[1]), bf16)
    aa[0:BASIS], aa[32:32 + BASIS] = bh, bl
    perm = np.zeros((nodes, nf * 128), np.float32)
    wrow = np.zeros((8, nf * 128), np.float32)
    for ea in range(count_a):
        for eb in range(EB):
            for ij in range(25):
                q = (ea * EB + eb) * 25 + ij
                spot = (q // nodes_mine) * 128 + q % nodes_mine
                perm[(ea * 25 + ij) * EB + eb, spot] = 1.0
                wrow[:, spot] = weights[ij]
    cfg = (nf, nm, own, R, wide, count_a, nodes, nb, start - rows, edge, orders, derive)
    vmem = pl.BlockSpec(memory_space=pltpu.VMEM)
    hbm = pl.BlockSpec(memory_space=pl.ANY)
    CW = rows_a.shape[1]
    steps = 2 * (2 * nb + 1)
    pairs, terms = -(-11 // steps) * steps, -(-21 // steps) * steps
    copies = 13 + 2 * nf
    field = jax.ShapeDtypeStruct((comps, rows, lanes), f32)
    forward_next, adjoint_next, sums = pl.pallas_call(
        functools.partial(core, cfg),
        out_shape=(field, field, jax.ShapeDtypeStruct(moduli.shape, f32)),
        in_specs=[hbm] * 8 + [vmem] * 7,
        out_specs=(vmem, vmem, vmem),
        scratch_shapes=[pltpu.VMEM((2 * W // 128, 4 * comps * R, 128), f32), pltpu.VMEM((12 * nodes, W), f32),
                        pltpu.VMEM((2 * pairs * nodes, CW), f32), pltpu.VMEM((terms * nodes, CW), f32),
                        pltpu.VMEM((terms, 32, nodes), f32), pltpu.VMEM((lanes * 128 // own, 256), bf16),
                        pltpu.VMEM((256, 256), bf16), pltpu.VMEM((256, 256), bf16),
                        pltpu.VMEM((2, 128, 2 * W), bf16),
                        pltpu.VMEM((2 * comps, rows, lanes), f32), pltpu.VMEM((2 * comps, rows, lanes), f32),
                        pltpu.VMEM((nf,) + flat.shape, f32), pltpu.VMEM((2 * pairs, 32, nf * 128), f32),
                        pltpu.VMEM((2 * comps, edge - 1, lanes), f32), pltpu.VMEM((2, R - HR, 128), f32),
                        pltpu.VMEM((2, R, 128), f32), pltpu.VMEM((2 * comps, rows, lanes), f32),
                        pltpu.VMEM((2 * comps, edge - 1, lanes), f32), pltpu.VMEM((2 * comps, edge - 1, lanes), f32),
                        pltpu.VMEM((2, R, 128), f32), pltpu.VMEM((2, R, 128), f32),
                        pltpu.VMEM((2, nf // 2) + flat.shape, f32), pltpu.VMEM((nf // 2,) + flat.shape, f32),
                        pltpu.VMEM((max(nf // 2 - 1, 1),) + flat.shape, f32),
                        pltpu.VMEM((nodes, 128), f32), pltpu.VMEM((-(-rows // 8) * 8, 128), f32),
                        pltpu.VMEM((2, own + halo, 2 * W), bf16), pltpu.VMEM((2, own + halo, 2 * W), bf16),
                        pltpu.VMEM(inner.shape, f32), pltpu.VMEM(fixes.shape, f32), pltpu.VMEM(perm.shape, bf16),
                        pltpu.VMEM((8, lanes), f32), pltpu.VMEM((8, lanes), f32),
                        pltpu.VMEM((8, lanes), f32), pltpu.VMEM((8, lanes), f32), pltpu.VMEM((comps * start, lanes), f32),
                        pltpu.SemaphoreType.DMA((8,)), pltpu.SemaphoreType.DMA((copies,)),
                        pltpu.SemaphoreType.DMA((copies,))],
        compiler_params=pltpu.CompilerParams(vmem_limit_bytes=60 * 1024 * 1024, collective_id=0,
                                             has_side_effects=True),
    )(forward_now, forward_last, adjoint_now, adjoint_last, flat, jnp.asarray(inner), jnp.asarray(fixes),
      jnp.asarray(perm.astype(bf16)), inv_radius.reshape(1, nodes), inv_mass.reshape(1, 2 * rows), jnp.asarray(a3), jnp.asarray(aa), jnp.asarray(wrow * (2.0 / n)),
      jnp.asarray(wrow * (kernel_weight * 2.0 * total / n)),
      jnp.asarray(np.broadcast_to(0.5 * waves(orders)[0][orders + ORD], (8, W)).astype(np.float32)))
    return forward_next, adjoint_next, sums


def solution(mesh):
    field = P(None, "meridian", "fourier")
    grid = P(None, None, "meridian", "fourier")
    in_specs = (field, field, field, field, grid, P("meridian"), P("meridian"))
    return jax.shard_map(body, mesh=mesh, in_specs=in_specs, out_specs=(field, field, grid),
                         check_vma=False)
```

```python
import functools
import math

import jax
import jax.numpy as jnp
import numpy as np
from jax import lax
from jax.experimental import pallas as pl
from jax.experimental.pallas import tpu as pltpu
from jax.sharding import PartitionSpec as P

ORD = 8
EB = 8
BASIS = 2 * ORD + 1
HR = (4 * EB + 2) // 2 // 8 * 8 + 8
MESH = pl.DeviceIdType.MESH
kernel_weight = 0.0001
bf16 = jnp.bfloat16
f32 = jnp.float32
PAIRS = [(a, b) for a in range(6) for b in range(a, 6)]
PART_A, PART_B, PART_P = (0, 5, 4), (5, 1, 3), (4, 3, 2)


def gll_tables():
    x = np.array([-1.0, -math.sqrt(3.0 / 7.0), 0.0, math.sqrt(3.0 / 7.0), 1.0])
    weights = np.array([0.1, 49.0 / 90.0, 32.0 / 45.0, 49.0 / 90.0, 0.1])
    factor = np.array([np.prod([x[i] - x[k] for k in range(5) if k != i]) for i in range(5)])
    derive = np.zeros((5, 5))
    for i in range(5):
        for k in range(5):
            if i != k:
                derive[i, k] = factor[i] / (factor[k] * (x[i] - x[k]))
            else:
                derive[i, k] = sum(1.0 / (x[i] - x[o]) for o in range(5) if o != i)
    return derive, np.outer(weights, weights).reshape(25)


def sample_count(orders):
    n = orders + 2 * ORD + 1
    return n, 0 if n <= 64 else -(-(n - 64) // 128)


def place(re, im, nb):
    cut, n = 128 * nb, re.shape[1]
    rest = np.zeros((re.shape[0], 128))
    head = np.zeros((2, re.shape[0], cut))
    wide = min(n, cut)
    head[0, :, :wide], head[1, :, :wide] = re[:, :wide], im[:, :wide]
    if n > cut:
        rest[:, :n - cut], rest[:, 64:64 + n - cut] = re[:, cut:], im[:, cut:]
    return np.concatenate([head[0], head[1], rest], axis=1)


def waves(orders):
    n, nb = sample_count(orders)
    at = np.arange(-ORD, orders + ORD + 1)
    turn = 2 * np.pi * ((at[:, None] * np.arange(n)[None, :]) % n) / n
    return place(np.cos(turn), np.sin(turn), nb), place(np.sin(turn), -np.cos(turn), nb)


def with_turned(table):
    turned = np.zeros_like(table)
    turned[0::2], turned[1::2] = -table[1::2], table[0::2]
    return np.concatenate([table, turned], axis=1).astype(np.float32)


def block_tables(orders, own):
    ec, es = waves(orders)
    inner = np.zeros((own + 4 * ORD, ec.shape[1]))
    for row, p in [(2 * p, p) for p in range(orders)] + [(own + 2 * i, i - ORD) for i in range(ORD)] \
            + [(own + 2 * ORD + 2 * i, orders + i) for i in range(ORD)]:
        inner[row], inner[row + 1] = 0.5 * ec[p + ORD], 0.5 * es[p + ORD]
    first, last = np.zeros_like(inner), np.zeros_like(inner)
    first[0], first[1] = 0.5 * ec[ORD], -inner[1]
    for p in range(1, ORD + 1):
        first[2 * p] += 0.5 * ec[ORD - p]
        first[2 * p + 1] -= 0.5 * es[ORD - p]
    first[own:own + 2 * ORD] = -inner[own:own + 2 * ORD]
    last[own + 2 * ORD:] = -inner[own + 2 * ORD:]
    last[own + 2 * ORD + 1] += ec[orders + ORD]
    for j in range(1, ORD + 1):
        last[2 * (orders - j)] += 0.5 * ec[orders + j + ORD]
        last[2 * (orders - j) + 1] -= 0.5 * es[orders + j + ORD]
    halo_last = np.zeros_like(inner)
    halo_last[own + 2 * ORD + 1] = 0.5 * ec[orders + ORD]
    return [with_turned(t) for t in (inner, first, last, halo_last)]


def basis_rows(orders):
    n, nb = sample_count(orders)
    j = np.arange(BASIS)[:, None]
    turn = ((j + 1) // 2) * (2 * np.pi * np.arange(n)[None, :] / n)
    rows = np.where((j % 2 == 0) & (j > 0), np.sin(turn), np.cos(turn))
    both = place(rows, rows, nb)
    return both[:, 128 * nb:]


def split_host(values):
    wide = np.asarray(values, np.float32)
    hi = wide.astype(bf16)
    return hi, (wide - hi.astype(np.float32)).astype(bf16)


def split_device(values):
    hi = lax.reduce_precision(values, 8, 7)
    return hi.astype(bf16), (values - hi).astype(bf16)


def split(values):
    hi = values.astype(bf16)
    return hi, (values - hi.astype(f32)).astype(bf16)


def nt(a, b):
    return lax.dot_general(a, b, (((1,), (1,)), ((), ())), preferred_element_type=f32)


def nn(a, b):
    return lax.dot_general(a, b, (((1,), (0,)), ((), ())), preferred_element_type=f32)


def line(matrix, u):
    s0, d0, s1, d1 = u[0] + u[4], u[0] - u[4], u[1] + u[3], u[1] - u[3]
    out = [None] * 5
    for i in range(2):
        m = [float(v) for v in matrix[i]]
        odd = (0.5 * (m[0] - m[4])) * d0 + (0.5 * (m[1] - m[3])) * d1
        even = (0.5 * (m[0] + m[4])) * s0 + (0.5 * (m[1] + m[3])) * s1 + m[2] * u[2]
        out[i], out[4 - i] = even + odd, odd - even
    m = [float(v) for v in matrix[2]]
    out[2] = m[0] * d0 + m[1] * d1
    return out


def core(cfg, fn_ref, an_ref, mod_ref, inner_ref, fix_ref, perm_in, rrow_ref, mrow_ref,
         a3_ref, aa_ref, wrow_ref, krow_ref, nyq_ref, f_ref, a_ref, k_ref,
         uz, es, cs, ps, accb, s_ref, s1_ref, s2_ref, t3_ref, xb, modr, modx, rh, stage, ring, force,
         edge_f, rm, spill, rspill, kb, kr, ks, rad_ref, mass_ref, tab_h, tab_l, inner_v, fix_v, perm_ref,
         pack, rpack, edge_p, rmp, x3, lsem, ssem, rsem):
    nf, nm, own, R, wide, count_a, nodes, nb, hrow, edge, own_orders, derive = cfg
    rows, lanes = fn_ref.shape[1:]
    W = 256 * nb + 128
    blocks = 2 * nb + 1
    halo = 4 * ORD
    main = R - HR
    tables = tuple((tab_h.at[l], tab_l.at[l]) for l in range(2))
    orders = own_orders
    me, mi = lax.axis_index("fourier"), lax.axis_index("meridian")
    up, down = lax.rem(me + 1, nf), lax.rem(me + nf - 1, nf)
    has_prev, has_next = mi > 0, mi < nm - 1
    is_last = jnp.where(me == nf - 1, 1.0, 0.0).astype(f32)

    def remote(src, dst, at, meridian, fourier):
        return pltpu.make_async_remote_copy(
            src_ref=src, dst_ref=dst, send_sem=ssem.at[at], recv_sem=rsem.at[at],
            device_id={"meridian": meridian, "fourier": fourier}, device_id_type=MESH)

    half = nf // 2
    odd = lax.rem(me, 2)
    partner, mine = me + 1 - 2 * odd, me // 2
    peers = [2 * lax.rem(mine + s + 1, half) + odd for s in range(half - 1)]
    sources = [2 * lax.rem(mine + half - 1 - s, half) + odd for s in range(half - 1)]
    first, top = pl.ds(0, HR), pl.ds(0, edge - 1)
    body_rows, tail_rows = pl.ds(0, main), pl.ds(main, HR)
    prev, nxt = mi - 1, mi + 1
    to_prev = [remote(fn_ref.at[:, top], rh.at[0:3], 0, prev, me),
               remote(an_ref.at[:, top], rh.at[3:6], 1, prev, me),
               remote(pack, rpack, 2, prev, me),
               remote(stage.at[0, first], ring.at[0, tail_rows], 3, prev, down),
               remote(stage.at[1, first], ring.at[1, tail_rows], 4, prev, up)]
    to_ring = [remote(stage.at[0], ring.at[0, body_rows], 5, mi, down),
               remote(stage.at[1], ring.at[1, body_rows], 6, mi, up)]
    to_next = [remote(edge_f, rm, 7, nxt, me), remote(edge_p, rmp, 8, nxt, me),
               remote(spill.at[0, tail_rows], rspill.at[0, tail_rows], 9, nxt, down),
               remote(spill.at[1, tail_rows], rspill.at[1, tail_rows], 10, nxt, up)]
    to_spill = [remote(spill.at[0, body_rows], rspill.at[0, body_rows], 11, mi, down),
                remote(spill.at[1, body_rows], rspill.at[1, body_rows], 12, mi, up)]
    base = 13
    mod_far = [remote(mod_ref, modr.at[me], base + s, mi, peers[s]) for s in range(half - 1)]
    mod_got = [remote(mod_ref, modr.at[sources[s]], base + s, mi, peers[s]) for s in range(half - 1)]
    base += half - 1
    mod_near = remote(mod_ref, modr.at[me], base, mi, partner)
    near_got = remote(mod_ref, modr.at[partner], base, mi, partner)
    mod_pass = [remote(modr.at[sources[s]], modr.at[sources[s]], base + 1 + s, mi, partner) for s in range(half - 1)]
    pass_got = [remote(modr.at[sources[s]], modr.at[sources[s] + 1 - 2 * odd], base + 1 + s, mi, partner)
                for s in range(half - 1)]
    base += half
    k_near = remote(kb.at[1 - odd], kr, base, mi, partner)
    k_far = [remote(kb.at[odd, lax.rem(mine + s + 1, half)], ks.at[s], base + 1 + s, mi, peers[s])
             for s in range(half - 1)]

    barrier = pltpu.get_barrier_semaphore()

    def greet(meridian, fourier):
        pl.semaphore_signal(barrier, inc=1, device_id={"meridian": meridian, "fourier": fourier},
                            device_id_type=MESH)

    for s in range(1, nf):
        greet(mi, lax.rem(me + s, nf))
    for there, other in ((has_prev, prev), (has_next, nxt)):
        @pl.when(there)
        def _(other=other):
            for f in (me, up, down):
                greet(other, f)

    loads = [pltpu.make_async_copy(an_ref, xb.at[3:6], lsem.at[0]), pltpu.make_async_copy(fn_ref, xb.at[0:3], lsem.at[1]),
             pltpu.make_async_copy(mod_ref, modr.at[me], lsem.at[2]),
             pltpu.make_async_copy(inner_ref, inner_v, lsem.at[3]), pltpu.make_async_copy(fix_ref, fix_v, lsem.at[4]),
             pltpu.make_async_copy(perm_in, perm_ref, lsem.at[5])]
    for copy in loads:
        copy.start()

    def onehot(shape, hit):
        a = lax.broadcasted_iota(jnp.int32, shape, 0)
        b = lax.broadcasted_iota(jnp.int32, shape, 1)
        return jnp.where(hit(a, b), 1.0, 0.0).astype(bf16)

    loads[0].wait()
    loads[1].wait()
    lane_id = lax.broadcasted_iota(jnp.int32, (rows, 128), 1)
    for way, source in enumerate((0, lanes - 128)):
        total = jnp.zeros((rows, 128), f32)
        for c in range(3):
            shift = (halo * c + (halo if way else 0)) % 128
            turned = xb[3 + c, :rows, source:source + 128]
            turned = pltpu.roll(turned, shift, 1) if shift else turned
            total = jnp.where((lane_id >= halo * c) & (lane_id < halo * (c + 1)), turned, total)
            if way == 0:
                turned = pltpu.roll(xb[c, :rows, :128], 3 * halo + 2 * c - 2, 1)
                spot = 3 * halo + 2 * c
                total = jnp.where((lane_id >= spot) & (lane_id < spot + 2), turned, total)
        stage[way, :rows] = total
        stage[way, rows:] = jnp.zeros((main - rows, 128), f32)

    for lc in range(6):
        pack[lc:lc + 1, :] = xb[lc, edge - 1:edge, :]
    pack[6:, :] = jnp.zeros((2, lanes), f32)
    pl.semaphore_wait(barrier, nf - 1 + 3 * (has_prev.astype(jnp.int32) + has_next.astype(jnp.int32)))

    @pl.when(has_prev)
    def _():
        for copy in to_prev:
            copy.start()
    for copy in to_ring + mod_far + [mod_near]:
        copy.start()

    lane8 = lax.broadcasted_iota(jnp.int32, (8, 128), 1)
    sub8 = lax.broadcasted_iota(jnp.int32, (8, 128), 0)

    def column(row_ref, lowest, highest, index):
        total = jnp.zeros((8, 128), f32)
        for b in range(lowest // 128, highest // 128 + 1):
            width = min(128, row_ref.shape[1] - 128 * b)
            values = jnp.broadcast_to(row_ref[0:1, 128 * b:128 * b + width], (8, width))
            if width < 128:
                values = jnp.concatenate([values, jnp.zeros((8, 128 - width), f32)], axis=1)
            total = total + jnp.where(lane8 + 128 * b == index, values, 0.0)
        return jnp.broadcast_to(jnp.sum(total, axis=1, keepdims=True), (8, 128))

    per_row = nodes // count_a
    for ea in range(count_a):
        for ij in range(25):
            at = (ea * 25 + ij) * 8
            rad_ref[at:at + 8, :] = column(rrow_ref, ea * per_row + ij, ea * per_row + ij + 25 * (EB - 1),
                                           25 * sub8 + (ea * per_row + ij))
    for i in range(-(-rows // 8)):
        high = min(16 * i + 15, mrow_ref.shape[1] - 1)
        mass_0 = column(mrow_ref, 16 * i, high, 2 * sub8 + 16 * i)
        mass_1 = column(mrow_ref, 16 * i, high, 2 * sub8 + (16 * i + 1))
        mass_ref[8 * i:8 * i + 8, :] = jnp.where(lane8 % 2 == 0, mass_0, mass_1)
    loads[3].wait()
    loads[4].wait()
    is_first = jnp.where(me == 0, 1.0, 0.0).astype(f32)
    sub16 = lax.broadcasted_iota(jnp.int32, (16, W), 0)
    start_order = (me * orders).astype(f32)

    def put_rows(ls, at, value, turn):
        h, lo = split(jnp.concatenate([value[:, :W], value[:, W:] * turn], axis=1))
        for l in ls:
            tab_h[l, pl.ds(at, 16)] = h
            tab_l[l, pl.ds(at, 16)] = lo

    def table_step(g, carry):
        at = pl.multiple_of(g * 16, 16)
        put_rows((0, 1), at, inner_v[pl.ds(at, 16), :], (8 * g + sub16 // 2).astype(f32) + start_order)
        return carry

    lax.fori_loop(0, own // 16, table_step, 0)
    for g in range(2):
        at, turn = 16 * g, (8 * g + sub16 // 2).astype(f32) + start_order
        put_rows((1,), at, inner_v[at:at + 16] + is_first * fix_v[at:at + 16], turn)
        put_rows((0,), at, inner_v[at:at + 16] + is_first * fix_v[32 + at:48 + at], turn)
        at, low = own + 16 * g, (orders if g else -ORD)
        turn = (low + sub16 // 2).astype(f32) + start_order
        if g:
            turn = jnp.where(sub16 < 2, turn * (1.0 - is_last), turn)
        put_rows((1,), at, inner_v[at:at + 16] + is_first * fix_v[80 + 16 * g:96 + 16 * g]
                 + is_last * fix_v[112 + 16 * g:128 + 16 * g], turn)
        put_rows((0,), at, is_last * fix_v[144 + 16 * g:160 + 16 * g], turn)
    at = 2 * orders - 16
    put_rows((1,), at, inner_v[at:at + 16] + is_last * fix_v[64:80],
             (at // 2 + sub16 // 2).astype(f32) + start_order)

    s_ref[...] = onehot(s_ref.shape, lambda a, b: (a % 2) * 128 + a // 2 == b)
    spot = lambda a: (a % 2) * 128 + (a // 128) * (2 * ORD) + (a % 128) // 2
    s1_ref[...] = onehot((256, 256), lambda a, b: (a % 128 < halo) & ((spot(a) == b) | (spot(a) + halo == b)))
    s2_ref[...] = onehot((256, 256), lambda a, b: (a % 128 < halo) & (spot(a) + 2 * halo == b))
    for l, (h, lo) in enumerate(tables):
        t3_ref[l, 0:halo] = h[own:]
        t3_ref[l, halo:2 * halo] = lo[own:]
        t3_ref[l, 2 * halo:3 * halo] = h[own:]
        t3_ref[l, 3 * halo:] = jnp.zeros((128 - 3 * halo, 2 * W), bf16)

    lane_blocks = own // 128
    bw = lanes // lane_blocks

    def apart(x):
        out = [nn(x[:, bw * b:bw * (b + 1)], s_ref[...]).astype(bf16) for b in range(lane_blocks)]
        return [jnp.concatenate([o[:, 128 * par:128 * (par + 1)] for o in out], axis=1) for par in range(2)]

    def samples(x, h_ref, l_ref, keep):
        xh, xl = split(x)
        hi, lo = apart(xh), apart(xl)
        for n in range(2 * W // 256):
            ln = slice(256 * n, 256 * (n + 1))
            for par in range(2):
                keep(par, n, nn(hi[par], h_ref[:own, ln]) + nn(hi[par], l_ref[:own, ln]) + nn(lo[par], h_ref[:own, ln]))

    def ahead(l, carry):
        def keep(par, n, out):
            for c in range(3):
                at = pl.ds(pl.multiple_of((2 * (3 * l + c) + par) * R, 8), main)
                for k in range(2):
                    uz[2 * n + k, at, :] = out[c * main:(c + 1) * main, 128 * k:128 * (k + 1)]
        for c in range(3):
            x3[c * main:c * main + rows, :] = xb[3 * l + c]
        samples(x3[...], tab_h.at[l], tab_l.at[l], keep)
        return carry

    lax.fori_loop(0, 2, ahead, 0)

    @pl.when(has_next)
    def _():
        for copy in to_prev:
            copy.wait_recv()

    @pl.when(jnp.logical_not(has_next))
    def _():
        rh[...] = jnp.zeros_like(rh)
        rpack[...] = jnp.zeros_like(rpack)
        ring[:, main:] = jnp.zeros((2, HR, 128), f32)
    for copy in to_ring:
        copy.wait_recv()
    for copy, forward in zip(mod_got, mod_pass):
        copy.wait_recv()
        forward.start()
    count = edge - 1
    for l, (h_ref, l_ref) in enumerate(tables):
        def keep(par, n, out, l=l):
            for c in range(3):
                at = (2 * (3 * l + c) + par) * R + main
                for k in range(2):
                    ln = slice(128 * k, 128 * (k + 1))
                    uz[2 * n + k, at:at + count, :] = out[c * count:(c + 1) * count, ln]
                    uz[2 * n + k, at + count:at + edge, :] = out[3 * count + 3 * l + c:3 * count + 3 * l + c + 1, ln]
        x = jnp.concatenate([rh[3 * l:3 * l + 3].reshape(3 * count, lanes), rpack[...]], axis=0)
        samples(x, h_ref, l_ref, keep)
    near = []
    for c in range(3):
        low, upper = ring[1], ring[0]
        if c:
            low, upper = pltpu.roll(low, 128 - halo * c, 1), pltpu.roll(upper, 128 - halo * c, 1)
        hh, hl = split(jnp.concatenate([low, upper], axis=1))
        he = (nn(hh, s1_ref[...]) + nn(hl, s2_ref[...])).astype(bf16)
        near += [he[:, :128], he[:, 128:]]
    near = jnp.concatenate(near, axis=0)
    for n in range(2 * W // 256):
        out = nn(near, t3_ref[1, :, 256 * n:256 * (n + 1)])
        for k in range(2):
            uz[2 * n + k, 6 * R:12 * R, :] += out[:, 128 * k:128 * (k + 1)]

    @pl.when(me == nf - 1)
    def _():
        for c in range(3):
            for par in range(2):
                spot = 3 * halo + 2 * c + par
                column = ring[0, :, spot:spot + 1]
                at = (2 * c + par) * R
                for b in range(blocks):
                    uz[b, at:at + R, :] += column * nyq_ref[0:1, 128 * b:128 * (b + 1)]

    loads[2].wait()
    near_got.wait_recv()
    for copy in pass_got:
        copy.wait_recv()
    loads[5].wait()
    modx[...] = jnp.zeros_like(modx)
    for r in range(21):
        for d in range(nf):
            ln = slice(128 * d, 128 * d + modr.shape[4])
            modx[r, :BASIS, ln] = modr[d, r, :, 0, :] * wrow_ref[0:1, ln]

    row_nodes, row_lanes = nodes // count_a, nf * 128 // count_a
    pairs_each = -(-11 // (2 * blocks))

    def moduli_pairs(ts):
        spread_out = []
        for t in ts:
            rows_two = []
            for k in range(2):
                h, lo = split(modx[2 * t + k])
                rows_two += [h, h, lo, jnp.zeros_like(h)]
            spread_out.append(jnp.concatenate(rows_two, axis=0))
        turned = []
        for ea in range(count_a):
            ln = slice(ea * row_lanes, (ea + 1) * row_lanes)
            for t, two in zip(ts, spread_out):
                mt = nt(perm_ref[ea * row_nodes:(ea + 1) * row_nodes, ln], two[:, ln]).astype(bf16)
                turned += [(t, k, ea, mt[:, 128 * k:128 * (k + 1)]) for k in range(2)]
        out = nn(jnp.concatenate([mt for _, _, _, mt in turned], axis=0), a3_ref[...])
        for i, (t, k, ea, _) in enumerate(turned):
            at = pl.multiple_of((2 * t + k) * nodes + ea * row_nodes, 8)
            cs[pl.ds(at, row_nodes), :] = out[i * row_nodes:(i + 1) * row_nodes]

    def point(a, j):
        p = wide * a + j
        return p % 2, p // 2 + (hrow if a == 4 * count_a else 0)

    def strain_step(t, carry):
        l, blk = t // blocks, t % blocks
        blk_z = blocks + blk

        def grid(c, ea, at_blk):
            out = []
            for i in range(5):
                row = []
                for j in range(5):
                    par, r = point(4 * ea + i, j)
                    at = (2 * (3 * l + c) + par) * R + r
                    row.append(uz[at_blk, pl.ds(at, 8, stride=2), :])
                out.append(row)
            return out

        def put(v, ea, i, j, value):
            row = v * nodes + ((ea * 5 + i) * 5 + j) * 8
            es[l, blk, row:row + 8, :] = value

        for ea in range(count_a):
            rad = lambda i, j: rad_ref[((ea * 5 + i) * 5 + j) * 8:((ea * 5 + i) * 5 + j) * 8 + 8, :]
            cols = lambda u: [[row[j] for row in u] for j in range(5)]
            u = grid(0, ea, blk)
            for j, col in enumerate(cols(u)):
                for i, v in enumerate(line(derive, col)):
                    put(0, ea, i, j, v)
            shear = [line(derive, row) for row in u]
            u = grid(1, ea, blk)
            for j, col in enumerate(cols(u)):
                for i, v in enumerate(line(derive, col)):
                    put(5, ea, i, j, v + shear[i][j])
            for i, row in enumerate(u):
                for j, v in enumerate(line(derive, row)):
                    put(1, ea, i, j, v)
            u = grid(2, ea, blk)
            z = grid(0, ea, blk_z)
            for j, col in enumerate(cols(u)):
                for i, v in enumerate(line(derive, col)):
                    put(4, ea, i, j, v + rad(i, j) * z[i][j])
            z = grid(1, ea, blk_z)
            for i, row in enumerate(u):
                for j, v in enumerate(line(derive, row)):
                    put(3, ea, i, j, v + rad(i, j) * z[i][j])
            z = grid(2, ea, blk_z)
            for i in range(5):
                for j in range(5):
                    put(2, ea, i, j, rad(i, j) * z[i][j])
        moduli_pairs([t * pairs_each + k for k in range(pairs_each)])
        return carry

    lax.fori_loop(0, 2 * blocks, strain_step, 0)

    def node_step(t, carry):
        row = pl.multiple_of(t * 8, 8)
        at = lambda v: pl.ds(pl.multiple_of(v * nodes + row, 8), 8)

        def add(sums, v, term):
            sums[v] = term if sums[v] is None else sums[v] + term

        def one(ce, els):
            fw = [[es[0, el, at(v), :] for v in range(6)] for el in els]
            ad = [[es[1, el, at(v), :] for v in range(6)] for el in els]
            sf = [[None] * 6 for _ in els]
            sa = [[None] * 6 for _ in els]
            for r, (v, w) in enumerate(PAIRS):
                c = cs[at(r), ce]
                total = None
                for f, a, tf, ta in zip(fw, ad, sf, sa):
                    add(tf, v, c * f[w])
                    add(ta, v, c * a[w])
                    if v != w:
                        add(tf, w, c * f[v])
                        add(ta, w, c * a[v])
                        prod = f[v] * a[w] + f[w] * a[v]
                    else:
                        prod = f[v] * a[v]
                    total = prod if total is None else total + prod
                ps[at(r), ce] = total
            for el, tf, ta in zip(els, sf, sa):
                for v in range(6):
                    es[0, el, at(v), :] = tf[v]
                    es[1, el, at(v), :] = ta[v]

        for b in range(nb):
            one(slice(128 * b, 128 * b + 128),
                [b, nb + b])
        one(slice(128 * nb, 128 * nb + 128), [2 * nb])
        return carry

    lax.fori_loop(0, nodes // 8, node_step, 0, unroll=2)

    each = -(-21 // (2 * blocks))

    def project(r):
        ph, plo = split(ps[pl.ds(pl.multiple_of(r * nodes, 8), nodes), :])
        both = nt(aa_ref[...], ph)
        accb[r] = both[:32] + both[32:] + nt(aa_ref[:32], plo)

    def force_step(t, carry):
        l, blk = t // blocks, t % blocks
        blk_z = blocks + blk
        top = lax.broadcasted_iota(jnp.int32, (8, 128), 0) == 0

        def get(v, ea, i, j):
            row = v * nodes + ((ea * 5 + i) * 5 + j) * 8
            return es[l, blk, row:row + 8, :]

        def store(c, a, row, at_blk):
            def where(j):
                par, r = point(a, j)
                return (2 * (3 * l + c) + par) * R + r
            for j in range(1, 4):
                uz[at_blk, pl.ds(where(j), 8, stride=2), :] = row[j]
            back = pltpu.roll(row[4], 1, 0)
            uz[at_blk, pl.ds(where(0), 8, stride=2), :] = row[0] + jnp.where(top, 0.0, back)
            uz[at_blk, pl.ds(where(4) + 14, 1), :] = row[4][7:8]

        beyond = wide * (4 * count_a + 1)
        for c in range(3):
            held, held_z = None, None
            spare = (2 * (3 * l + c) + beyond % 2) * R + beyond // 2 + hrow
            for b in (blk, blk_z):
                uz[b, pl.ds(spare, 1), :] = jnp.zeros((1, 128), f32)
            for ea in range(count_a):
                rad = lambda i, j: rad_ref[((ea * 5 + i) * 5 + j) * 8:((ea * 5 + i) * 5 + j) * 8 + 8, :]
                cols = [line(derive.T, [get(PART_A[c], ea, i, j) for i in range(5)]) for j in range(5)]
                for i in range(5):
                    row = line(derive.T, [get(PART_B[c], ea, i, j) for j in range(5)])
                    row = [row[j] + cols[j][i] for j in range(5)]
                    row_z = [rad(i, j) * get(PART_P[c], ea, i, j) for j in range(5)]
                    if i == 0 and held is not None:
                        row = [p + q for p, q in zip(row, held)]
                        row_z = [p + q for p, q in zip(row_z, held_z)]
                    if i == 4 and ea + 1 < count_a:
                        held, held_z = row, row_z
                    else:
                        store(c, 4 * ea + i, row, blk)
                        store(c, 4 * ea + i, row_z, blk_z)
        for k in range(each):
            project(t * each + k)
        return carry

    lax.fori_loop(0, 2 * blocks, force_step, 0)
    h, lo = split(accb[:21].reshape(21 * 32, nodes))
    for ea in range(count_a):
        q, ln = slice(ea * row_nodes, (ea + 1) * row_nodes), slice(ea * row_lanes, (ea + 1) * row_lanes)
        part = (nn(h[:, q], perm_ref[q, ln]) + nn(lo[:, q], perm_ref[q, ln])) * krow_ref[0:1, ln]
        for k in range(nf // count_a):
            for r in range(21):
                d = ea * (nf // count_a) + k
                kb[d % 2, d // 2, r * BASIS:(r + 1) * BASIS, :] = \
                    part[32 * r:32 * r + BASIS, 128 * k:128 * k + kb.shape[3]]
    k_near.start()

    def interleave(both):
        out = []
        for b in range(lane_blocks):
            ln = slice(128 * b, 128 * (b + 1))
            h, lo = split(jnp.concatenate([both[0][:, ln], both[1][:, ln]], axis=1))
            out.append(nt(h, s_ref[...]) + nt(lo, s_ref[...]))
        return jnp.concatenate(out, axis=1)

    def turn_back(parts, l, with_edge):
        h_ref, l_ref = tables[1 - l]
        both, edge_h, edge_l = [], [], []
        for part in parts:
            h, lo = split(part)
            both.append(nt(h, h_ref[:own]) + nt(h, l_ref[:own]) + nt(lo, h_ref[:own]))
            if with_edge:
                edge_h.append(nt(h, t3_ref[1 - l]))
                edge_l.append(nt(lo, t3_ref[1 - l]))
        out = interleave(both)
        if not with_edge:
            return out, None
        h, lo = split(jnp.concatenate(edge_h, axis=1))
        side = nt(h, s1_ref[...]) + nt(lo, s1_ref[...])
        h, lo = split(jnp.concatenate(edge_l, axis=1))
        return out, side + nt(h, s2_ref[...]) + nt(lo, s2_ref[...])

    def spread(side, c):
        low, high = side[:, :128], side[:, 128:]
        return (pltpu.roll(low, halo * c, 1), pltpu.roll(high, halo * c, 1)) if c else (low, high)

    def read(lc, par, start, count):
        at = (2 * lc + par) * R + start
        return jnp.concatenate([uz[b, at:at + count, :] for b in range(2 * blocks)], axis=1)

    high = jnp.zeros((R, 128), f32)
    lane_r = lax.broadcasted_iota(jnp.int32, (R, 128), 1)
    for c in range(3):
        for par in range(2):
            at = (2 * (3 + c) + par) * R
            terms = None
            for b in range(blocks):
                term = uz[b, at:at + R, :] * nyq_ref[0:1, 128 * b:128 * (b + 1)]
                terms = term if terms is None else terms + term
            value = jnp.sum(terms, axis=1, keepdims=True) * is_last
            high = jnp.where(lane_r == 3 * halo + 2 * c + par, value, high)
    spill[0] = jnp.zeros((R, 128), f32)
    spill[1] = high

    for l in range(2):
        parts = [jnp.concatenate([read(3 * l + c, par, main, HR) for c in range(3)], axis=0) for par in range(2)]
        out, side = turn_back(parts, l, l == 0)
        for c in range(3):
            edge_f[3 * l + c] = out[c * HR:c * HR + count]
            edge_p[3 * l + c:3 * l + c + 1, :] = out[c * HR + count:c * HR + edge]
        if l == 0:
            for c in range(3):
                for way, value in enumerate(spread(side[c * HR:(c + 1) * HR], c)):
                    spill[way, main:] += value

    edge_p[6:, :] = jnp.zeros((2, lanes), f32)

    @pl.when(has_next)
    def _():
        for copy in to_next:
            copy.start()
    k_near.wait_recv()
    k_near.wait_send()
    kb[odd] += kr[...]
    for copy in k_far:
        copy.start()
    for c in range(3):
        out, side = turn_back([read(c, par, 0, main) for par in range(2)], 0, True)
        force[c] = out[:rows]
        for way, value in enumerate(spread(side, c)):
            spill[way, :main] += value
    for copy in to_spill:
        copy.start()

    def adjoint_back(c, carry):
        at = [pl.ds(pl.multiple_of((2 * (3 + c) + par) * R, 8), main) for par in range(2)]
        parts = [jnp.concatenate([uz[b, a, :] for b in range(2 * blocks)], axis=1) for a in at]
        out, _ = turn_back(parts, 1, False)
        force[3 + c] = out[:rows]
        return carry

    lax.fori_loop(0, 3, adjoint_back, 0)

    lane_m = lax.broadcasted_iota(jnp.int32, (rows, 128), 1)

    def gather(start, count):
        for c in range(3):
            up_turned = rspill[1, start:start + count]
            up_turned = pltpu.roll(up_turned, 128 - halo * c, 1) if c else up_turned
            force[c, :count, :128] += jnp.where(lane_m[:count] < halo, up_turned, 0.0)
            low_turned = pltpu.roll(rspill[0, start:start + count], (128 - halo * (c + 1)), 1)
            force[c, :count, lanes - 128:] += jnp.where(lane_m[:count] >= 128 - halo, low_turned, 0.0)
            top_turned = pltpu.roll(rspill[1, start:start + count], 128 - 3 * halo - 2 * c + 2, 1)
            force[3 + c, :count, :128] += jnp.where((lane_m[:count] >= 2) & (lane_m[:count] < 4), top_turned, 0.0)

    @pl.when(has_prev)
    def _():
        for copy in to_next:
            copy.wait_recv()
        force[:, :edge - 1] += rm[...]
        for lc in range(6):
            force[lc, edge - 1:edge, :] += rmp[lc:lc + 1, :]
        gather(main, edge)
    for copy in to_spill:
        copy.wait_recv()
    gather(0, rows)
    mass = jnp.concatenate([mass_ref[:rows]] * (lanes // 128), axis=1)
    for c in range(3):
        f_ref[c] = mass * force[c]
        a_ref[c] = mass * force[3 + c]
    for copy in k_far:
        copy.wait_recv()
    total = kb[odd, mine]
    for s in range(half - 1):
        total = total + ks[s]
    for r in range(21):
        k_ref[r, :, 0, :] = total[r * BASIS:(r + 1) * BASIS]

    @pl.when(has_prev)
    def _():
        for copy in to_prev:
            copy.wait_send()

    @pl.when(has_next)
    def _():
        for copy in to_next:
            copy.wait_send()
    for copy in to_ring + to_spill + mod_far + [mod_near] + mod_pass + k_far:
        copy.wait_send()


def body(forward_now, forward_last, adjoint_now, adjoint_last, moduli, inv_radius, inv_mass):
    derive, weights = gll_tables()
    wide = 4 * EB + 1
    nf = lax.axis_size("fourier")
    nm = lax.axis_size("meridian")
    me = lax.axis_index("fourier")
    comps, rows, lanes = forward_now.shape
    local = lanes // 2
    total = local * nf
    orders = local // 2
    own = -(-local // 128) * 128
    row_count = 2 * rows // wide
    count_a = row_count // 4
    nodes_mine = moduli.shape[3]
    nodes = nodes_mine * nf
    edge = (wide + 1) // 2
    start = -(-rows // 8) * 8
    R = start + HR
    n, nb = sample_count(orders)
    W = 256 * nb + 128
    halo = 4 * ORD

    flat = jax.ShapeDtypeStruct((21 * BASIS, nodes_mine), f32)

    inner, first, last, halo_last = block_tables(orders, own)
    drop = np.zeros_like(first[:32])
    drop[:] = with_turned(np.where(np.arange(32)[:, None] == 1, -inner[:32, :W], 0.0))
    fixes = np.concatenate([first[:32], drop, last[local - 16:local], first[own:], last[own:], halo_last[own:]], axis=0)

    rows_a = basis_rows(orders)
    bh, bl = split_host(rows_a)
    a3 = np.zeros((128, rows_a.shape[1]), bf16)
    a3[0:BASIS], a3[32:32 + BASIS], a3[64:64 + BASIS] = bh, bl, bh
    aa = np.zeros((64, rows_a.shape[1]), bf16)
    aa[0:BASIS], aa[32:32 + BASIS] = bh, bl
    perm = np.zeros((nodes, nf * 128), np.float32)
    wrow = np.zeros((8, nf * 128), np.float32)
    for ea in range(count_a):
        for eb in range(EB):
            for ij in range(25):
                q = (ea * EB + eb) * 25 + ij
                spot = (q // nodes_mine) * 128 + q % nodes_mine
                perm[(ea * 25 + ij) * EB + eb, spot] = 1.0
                wrow[:, spot] = weights[ij]
    cfg = (nf, nm, own, R, wide, count_a, nodes, nb, start - rows, edge, orders, derive)
    vmem = pl.BlockSpec(memory_space=pltpu.VMEM)
    hbm = pl.BlockSpec(memory_space=pl.ANY)
    CW = rows_a.shape[1]
    steps = 2 * (2 * nb + 1)
    pairs, terms = -(-11 // steps) * steps, -(-21 // steps) * steps
    copies = 13 + 2 * nf
    field = jax.ShapeDtypeStruct((comps, rows, lanes), f32)
    force_f, force_a, sums = pl.pallas_call(
        functools.partial(core, cfg),
        out_shape=(field, field, jax.ShapeDtypeStruct(moduli.shape, f32)),
        in_specs=[hbm] * 6 + [vmem] * 7,
        out_specs=(vmem, vmem, vmem),
        scratch_shapes=[pltpu.VMEM((2 * W // 128, 4 * comps * R, 128), f32), pltpu.VMEM((2, W // 128, 6 * nodes, 128), f32),
                        pltpu.VMEM((2 * pairs * nodes, CW), f32), pltpu.VMEM((terms * nodes, CW), f32),
                        pltpu.VMEM((terms, 32, nodes), f32), pltpu.VMEM((lanes * 128 // own, 256), bf16),
                        pltpu.VMEM((256, 256), bf16), pltpu.VMEM((256, 256), bf16),
                        pltpu.VMEM((2, 128, 2 * W), bf16),
                        pltpu.VMEM((2 * comps, rows, lanes), f32),
                        pltpu.VMEM((nf,) + moduli.shape, f32), pltpu.VMEM((2 * pairs, 32, nf * 128), f32),
                        pltpu.VMEM((2 * comps, edge - 1, lanes), f32), pltpu.VMEM((2, R - HR, 128), f32),
                        pltpu.VMEM((2, R, 128), f32), pltpu.VMEM((2 * comps, rows, lanes), f32),
                        pltpu.VMEM((2 * comps, edge - 1, lanes), f32), pltpu.VMEM((2 * comps, edge - 1, lanes), f32),
                        pltpu.VMEM((2, R, 128), f32), pltpu.VMEM((2, R, 128), f32),
                        pltpu.VMEM((2, nf // 2) + flat.shape, f32), pltpu.VMEM((nf // 2,) + flat.shape, f32),
                        pltpu.VMEM((max(nf // 2 - 1, 1),) + flat.shape, f32),
                        pltpu.VMEM((nodes, 128), f32), pltpu.VMEM((-(-rows // 8) * 8, 128), f32),
                        pltpu.VMEM((2, own + halo, 2 * W), bf16), pltpu.VMEM((2, own + halo, 2 * W), bf16),
                        pltpu.VMEM(inner.shape, f32), pltpu.VMEM(fixes.shape, f32), pltpu.VMEM(perm.shape, bf16),
                        pltpu.VMEM((8, lanes), f32), pltpu.VMEM((8, lanes), f32),
                        pltpu.VMEM((8, lanes), f32), pltpu.VMEM((8, lanes), f32), pltpu.VMEM((comps * start, lanes), f32),
                        pltpu.SemaphoreType.DMA((6,)), pltpu.SemaphoreType.DMA((copies,)),
                        pltpu.SemaphoreType.DMA((copies,))],
        compiler_params=pltpu.CompilerParams(vmem_limit_bytes=60 * 1024 * 1024, collective_id=0,
                                             has_side_effects=True),
    )(forward_now, adjoint_now, moduli, jnp.asarray(inner), jnp.asarray(fixes),
      jnp.asarray(perm.astype(bf16)), inv_radius.reshape(1, nodes), inv_mass.reshape(1, 2 * rows), jnp.asarray(a3), jnp.asarray(aa), jnp.asarray(wrow * (2.0 / n)),
      jnp.asarray(wrow * (kernel_weight * 2.0 * total / n)),
      jnp.asarray(np.broadcast_to(0.5 * waves(orders)[0][orders + ORD], (8, W)).astype(np.float32)))
    return 2.0 * forward_now - forward_last - force_f, 2.0 * adjoint_now - adjoint_last - force_a, sums


def solution(mesh):
    field = P(None, "meridian", "fourier")
    grid = P(None, None, "meridian", "fourier")
    in_specs = (field, field, field, field, grid, P("meridian"), P("meridian"))
    return jax.shard_map(body, mesh=mesh, in_specs=in_specs, out_specs=(field, field, grid),
                         check_vma=False)
```

```python
import functools
import math

import jax
import jax.numpy as jnp
import numpy as np
from jax import lax
from jax.experimental import pallas as pl
from jax.experimental.pallas import tpu as pltpu
from jax.sharding import PartitionSpec as P

ORD = 8
EB = 8
BASIS = 2 * ORD + 1
HR = (4 * EB + 2) // 2 // 8 * 8 + 8
MESH = pl.DeviceIdType.MESH
kernel_weight = 0.0001
bf16 = jnp.bfloat16
f32 = jnp.float32
PAIRS = [(a, b) for a in range(6) for b in range(a, 6)]
PART_A, PART_B, PART_P = (0, 5, 4), (5, 1, 3), (4, 3, 2)


def gll_tables():
    x = np.array([-1.0, -math.sqrt(3.0 / 7.0), 0.0, math.sqrt(3.0 / 7.0), 1.0])
    weights = np.array([0.1, 49.0 / 90.0, 32.0 / 45.0, 49.0 / 90.0, 0.1])
    factor = np.array([np.prod([x[i] - x[k] for k in range(5) if k != i]) for i in range(5)])
    derive = np.zeros((5, 5))
    for i in range(5):
        for k in range(5):
            if i != k:
                derive[i, k] = factor[i] / (factor[k] * (x[i] - x[k]))
            else:
                derive[i, k] = sum(1.0 / (x[i] - x[o]) for o in range(5) if o != i)
    return derive, np.outer(weights, weights).reshape(25)


def sample_count(orders):
    n = orders + 2 * ORD + 1
    return n, 0 if n <= 64 else -(-(n - 64) // 128)


def place(re, im, nb):
    cut, n = 128 * nb, re.shape[1]
    rest = np.zeros((re.shape[0], 128))
    head = np.zeros((2, re.shape[0], cut))
    wide = min(n, cut)
    head[0, :, :wide], head[1, :, :wide] = re[:, :wide], im[:, :wide]
    if n > cut:
        rest[:, :n - cut], rest[:, 64:64 + n - cut] = re[:, cut:], im[:, cut:]
    return np.concatenate([head[0], head[1], rest], axis=1)


def waves(orders):
    n, nb = sample_count(orders)
    at = np.arange(-ORD, orders + ORD + 1)
    turn = 2 * np.pi * ((at[:, None] * np.arange(n)[None, :]) % n) / n
    return place(np.cos(turn), np.sin(turn), nb), place(np.sin(turn), -np.cos(turn), nb)


def with_turned(table):
    turned = np.zeros_like(table)
    turned[0::2], turned[1::2] = -table[1::2], table[0::2]
    return np.concatenate([table, turned], axis=1).astype(np.float32)


def block_tables(orders, own):
    ec, es = waves(orders)
    inner = np.zeros((own + 4 * ORD, ec.shape[1]))
    for row, p in [(2 * p, p) for p in range(orders)] + [(own + 2 * i, i - ORD) for i in range(ORD)] \
            + [(own + 2 * ORD + 2 * i, orders + i) for i in range(ORD)]:
        inner[row], inner[row + 1] = 0.5 * ec[p + ORD], 0.5 * es[p + ORD]
    first, last = np.zeros_like(inner), np.zeros_like(inner)
    first[0], first[1] = 0.5 * ec[ORD], -inner[1]
    for p in range(1, ORD + 1):
        first[2 * p] += 0.5 * ec[ORD - p]
        first[2 * p + 1] -= 0.5 * es[ORD - p]
    first[own:own + 2 * ORD] = -inner[own:own + 2 * ORD]
    last[own + 2 * ORD:] = -inner[own + 2 * ORD:]
    last[own + 2 * ORD + 1] += ec[orders + ORD]
    for j in range(1, ORD + 1):
        last[2 * (orders - j)] += 0.5 * ec[orders + j + ORD]
        last[2 * (orders - j) + 1] -= 0.5 * es[orders + j + ORD]
    halo_last = np.zeros_like(inner)
    halo_last[own + 2 * ORD + 1] = 0.5 * ec[orders + ORD]
    return [with_turned(t) for t in (inner, first, last, halo_last)]


def basis_rows(orders):
    n, nb = sample_count(orders)
    j = np.arange(BASIS)[:, None]
    turn = ((j + 1) // 2) * (2 * np.pi * np.arange(n)[None, :] / n)
    rows = np.where((j % 2 == 0) & (j > 0), np.sin(turn), np.cos(turn))
    both = place(rows, rows, nb)
    return both[:, 128 * nb:]


def split_host(values):
    wide = np.asarray(values, np.float32)
    hi = wide.astype(bf16)
    return hi, (wide - hi.astype(np.float32)).astype(bf16)


def split_device(values):
    hi = lax.reduce_precision(values, 8, 7)
    return hi.astype(bf16), (values - hi).astype(bf16)


def split(values):
    hi = values.astype(bf16)
    return hi, (values - hi.astype(f32)).astype(bf16)


def nt(a, b):
    return lax.dot_general(a, b, (((1,), (1,)), ((), ())), preferred_element_type=f32)


def nn(a, b):
    return lax.dot_general(a, b, (((1,), (0,)), ((), ())), preferred_element_type=f32)


def line(matrix, u):
    s0, d0, s1, d1 = u[0] + u[4], u[0] - u[4], u[1] + u[3], u[1] - u[3]
    out = [None] * 5
    for i in range(2):
        m = [float(v) for v in matrix[i]]
        odd = (0.5 * (m[0] - m[4])) * d0 + (0.5 * (m[1] - m[3])) * d1
        even = (0.5 * (m[0] + m[4])) * s0 + (0.5 * (m[1] + m[3])) * s1 + m[2] * u[2]
        out[i], out[4 - i] = even + odd, odd - even
    m = [float(v) for v in matrix[2]]
    out[2] = m[0] * d0 + m[1] * d1
    return out


def core(cfg, fn_ref, an_ref, mod_ref, inner_ref, fix_ref, perm_in, rrow_ref, mrow_ref,
         a3_ref, aa_ref, wrow_ref, krow_ref, nyq_ref, f_ref, a_ref, k_ref,
         uz, es, cs, ps, accb, s_ref, s1_ref, s2_ref, t3_ref, xb, modr, modx, rh, stage, ring, force,
         edge_f, rm, spill, rspill, kb, kr, ks, rad_ref, mass_ref, tab_h, tab_l, inner_v, fix_v, perm_ref,
         pack, rpack, edge_p, rmp, x3, lsem, ssem, rsem):
    nf, nm, own, R, wide, count_a, nodes, nb, hrow, edge, own_orders, derive = cfg
    rows, lanes = fn_ref.shape[1:]
    W = 256 * nb + 128
    blocks = 2 * nb + 1
    halo = 4 * ORD
    main = R - HR
    tables = tuple((tab_h.at[l], tab_l.at[l]) for l in range(2))
    orders = own_orders
    me, mi = lax.axis_index("fourier"), lax.axis_index("meridian")
    up, down = lax.rem(me + 1, nf), lax.rem(me + nf - 1, nf)
    has_prev, has_next = mi > 0, mi < nm - 1
    is_last = jnp.where(me == nf - 1, 1.0, 0.0).astype(f32)

    def remote(src, dst, at, meridian, fourier):
        return pltpu.make_async_remote_copy(
            src_ref=src, dst_ref=dst, send_sem=ssem.at[at], recv_sem=rsem.at[at],
            device_id={"meridian": meridian, "fourier": fourier}, device_id_type=MESH)

    half = nf // 2
    odd = lax.rem(me, 2)
    partner, mine = me + 1 - 2 * odd, me // 2
    peers = [2 * lax.rem(mine + s + 1, half) + odd for s in range(half - 1)]
    sources = [2 * lax.rem(mine + half - 1 - s, half) + odd for s in range(half - 1)]
    first, top = pl.ds(0, HR), pl.ds(0, edge - 1)
    body_rows, tail_rows = pl.ds(0, main), pl.ds(main, HR)
    prev, nxt = mi - 1, mi + 1
    to_prev = [remote(fn_ref.at[:, top], rh.at[0:3], 0, prev, me),
               remote(an_ref.at[:, top], rh.at[3:6], 1, prev, me),
               remote(pack, rpack, 2, prev, me),
               remote(stage.at[0, first], ring.at[0, tail_rows], 3, prev, down),
               remote(stage.at[1, first], ring.at[1, tail_rows], 4, prev, up)]
    to_ring = [remote(stage.at[0], ring.at[0, body_rows], 5, mi, down),
               remote(stage.at[1], ring.at[1, body_rows], 6, mi, up)]
    to_next = [remote(edge_f, rm, 7, nxt, me), remote(edge_p, rmp, 8, nxt, me),
               remote(spill.at[0, tail_rows], rspill.at[0, tail_rows], 9, nxt, down),
               remote(spill.at[1, tail_rows], rspill.at[1, tail_rows], 10, nxt, up)]
    to_spill = [remote(spill.at[0, body_rows], rspill.at[0, body_rows], 11, mi, down),
                remote(spill.at[1, body_rows], rspill.at[1, body_rows], 12, mi, up)]
    base = 13
    mod_far = [remote(mod_ref, modr.at[me], base + s, mi, peers[s]) for s in range(half - 1)]
    mod_got = [remote(mod_ref, modr.at[sources[s]], base + s, mi, peers[s]) for s in range(half - 1)]
    base += half - 1
    mod_near = remote(mod_ref, modr.at[me], base, mi, partner)
    near_got = remote(mod_ref, modr.at[partner], base, mi, partner)
    mod_pass = [remote(modr.at[sources[s]], modr.at[sources[s]], base + 1 + s, mi, partner) for s in range(half - 1)]
    pass_got = [remote(modr.at[sources[s]], modr.at[sources[s] + 1 - 2 * odd], base + 1 + s, mi, partner)
                for s in range(half - 1)]
    base += half
    k_near = remote(kb.at[1 - odd], kr, base, mi, partner)
    k_far = [remote(kb.at[odd, lax.rem(mine + s + 1, half)], ks.at[s], base + 1 + s, mi, peers[s])
             for s in range(half - 1)]

    barrier = pltpu.get_barrier_semaphore()

    def greet(meridian, fourier):
        pl.semaphore_signal(barrier, inc=1, device_id={"meridian": meridian, "fourier": fourier},
                            device_id_type=MESH)

    for s in range(1, nf):
        greet(mi, lax.rem(me + s, nf))
    for there, other in ((has_prev, prev), (has_next, nxt)):
        @pl.when(there)
        def _(other=other):
            for f in (me, up, down):
                greet(other, f)

    loads = [pltpu.make_async_copy(an_ref, xb.at[3:6], lsem.at[0]), pltpu.make_async_copy(fn_ref, xb.at[0:3], lsem.at[1]),
             pltpu.make_async_copy(mod_ref, modr.at[me], lsem.at[2]),
             pltpu.make_async_copy(inner_ref, inner_v, lsem.at[3]), pltpu.make_async_copy(fix_ref, fix_v, lsem.at[4]),
             pltpu.make_async_copy(perm_in, perm_ref, lsem.at[5])]
    for copy in loads:
        copy.start()

    def onehot(shape, hit):
        a = lax.broadcasted_iota(jnp.int32, shape, 0)
        b = lax.broadcasted_iota(jnp.int32, shape, 1)
        return jnp.where(hit(a, b), 1.0, 0.0).astype(bf16)

    loads[0].wait()
    loads[1].wait()
    lane_id = lax.broadcasted_iota(jnp.int32, (rows, 128), 1)
    for way, source in enumerate((0, lanes - 128)):
        total = jnp.zeros((rows, 128), f32)
        for c in range(3):
            shift = (halo * c + (halo if way else 0)) % 128
            turned = xb[3 + c, :rows, source:source + 128]
            turned = pltpu.roll(turned, shift, 1) if shift else turned
            total = jnp.where((lane_id >= halo * c) & (lane_id < halo * (c + 1)), turned, total)
            if way == 0:
                turned = pltpu.roll(xb[c, :rows, :128], 3 * halo + 2 * c - 2, 1)
                spot = 3 * halo + 2 * c
                total = jnp.where((lane_id >= spot) & (lane_id < spot + 2), turned, total)
        stage[way, :rows] = total
        stage[way, rows:] = jnp.zeros((main - rows, 128), f32)

    for lc in range(6):
        pack[lc:lc + 1, :] = xb[lc, edge - 1:edge, :]
    pack[6:, :] = jnp.zeros((2, lanes), f32)
    pl.semaphore_wait(barrier, nf - 1 + 3 * (has_prev.astype(jnp.int32) + has_next.astype(jnp.int32)))

    for copy in to_ring:
        copy.start()

    @pl.when(has_prev)
    def _():
        for copy in to_prev[::-1]:
            copy.start()
    for copy in mod_far + [mod_near]:
        copy.start()

    lane8 = lax.broadcasted_iota(jnp.int32, (8, 128), 1)
    sub8 = lax.broadcasted_iota(jnp.int32, (8, 128), 0)

    def column(row_ref, lowest, highest, index):
        total = jnp.zeros((8, 128), f32)
        for b in range(lowest // 128, highest // 128 + 1):
            width = min(128, row_ref.shape[1] - 128 * b)
            values = jnp.broadcast_to(row_ref[0:1, 128 * b:128 * b + width], (8, width))
            if width < 128:
                values = jnp.concatenate([values, jnp.zeros((8, 128 - width), f32)], axis=1)
            total = total + jnp.where(lane8 + 128 * b == index, values, 0.0)
        return jnp.broadcast_to(jnp.sum(total, axis=1, keepdims=True), (8, 128))

    per_row = nodes // count_a
    for ea in range(count_a):
        for ij in range(25):
            at = (ea * 25 + ij) * 8
            rad_ref[at:at + 8, :] = column(rrow_ref, ea * per_row + ij, ea * per_row + ij + 25 * (EB - 1),
                                           25 * sub8 + (ea * per_row + ij))
    for i in range(-(-rows // 8)):
        high = min(16 * i + 15, mrow_ref.shape[1] - 1)
        mass_0 = column(mrow_ref, 16 * i, high, 2 * sub8 + 16 * i)
        mass_1 = column(mrow_ref, 16 * i, high, 2 * sub8 + (16 * i + 1))
        mass_ref[8 * i:8 * i + 8, :] = jnp.where(lane8 % 2 == 0, mass_0, mass_1)
    loads[3].wait()
    loads[4].wait()
    is_first = jnp.where(me == 0, 1.0, 0.0).astype(f32)
    sub16 = lax.broadcasted_iota(jnp.int32, (16, W), 0)
    start_order = (me * orders).astype(f32)

    def put_rows(ls, at, value, turn):
        h, lo = split(jnp.concatenate([value[:, :W], value[:, W:] * turn], axis=1))
        for l in ls:
            tab_h[l, pl.ds(at, 16)] = h
            tab_l[l, pl.ds(at, 16)] = lo

    def table_step(g, carry):
        at = pl.multiple_of(g * 16, 16)
        put_rows((0, 1), at, inner_v[pl.ds(at, 16), :], (8 * g + sub16 // 2).astype(f32) + start_order)
        return carry

    lax.fori_loop(0, own // 16, table_step, 0)
    for g in range(2):
        at, turn = 16 * g, (8 * g + sub16 // 2).astype(f32) + start_order
        put_rows((1,), at, inner_v[at:at + 16] + is_first * fix_v[at:at + 16], turn)
        put_rows((0,), at, inner_v[at:at + 16] + is_first * fix_v[32 + at:48 + at], turn)
        at, low = own + 16 * g, (orders if g else -ORD)
        turn = (low + sub16 // 2).astype(f32) + start_order
        if g:
            turn = jnp.where(sub16 < 2, turn * (1.0 - is_last), turn)
        put_rows((1,), at, inner_v[at:at + 16] + is_first * fix_v[80 + 16 * g:96 + 16 * g]
                 + is_last * fix_v[112 + 16 * g:128 + 16 * g], turn)
        put_rows((0,), at, is_last * fix_v[144 + 16 * g:160 + 16 * g], turn)
    at = 2 * orders - 16
    put_rows((1,), at, inner_v[at:at + 16] + is_last * fix_v[64:80],
             (at // 2 + sub16 // 2).astype(f32) + start_order)

    s_ref[...] = onehot(s_ref.shape, lambda a, b: (a % 2) * 128 + a // 2 == b)
    spot = lambda a: (a % 2) * 128 + (a // 128) * (2 * ORD) + (a % 128) // 2
    s1_ref[...] = onehot((256, 256), lambda a, b: (a % 128 < halo) & ((spot(a) == b) | (spot(a) + halo == b)))
    s2_ref[...] = onehot((256, 256), lambda a, b: (a % 128 < halo) & (spot(a) + 2 * halo == b))
    for l, (h, lo) in enumerate(tables):
        t3_ref[l, 0:halo] = h[own:]
        t3_ref[l, halo:2 * halo] = lo[own:]
        t3_ref[l, 2 * halo:3 * halo] = h[own:]
        t3_ref[l, 3 * halo:] = jnp.zeros((128 - 3 * halo, 2 * W), bf16)

    lane_blocks = own // 128
    bw = lanes // lane_blocks

    def apart(x):
        out = [nn(x[:, bw * b:bw * (b + 1)], s_ref[...]).astype(bf16) for b in range(lane_blocks)]
        return [jnp.concatenate([o[:, 128 * par:128 * (par + 1)] for o in out], axis=1) for par in range(2)]

    def samples(x, h_ref, l_ref, keep):
        xh, xl = split(x)
        hi, lo = apart(xh), apart(xl)
        for n in range(2 * W // 256):
            ln = slice(256 * n, 256 * (n + 1))
            for par in range(2):
                keep(par, n, nn(hi[par], h_ref[:own, ln]) + nn(hi[par], l_ref[:own, ln]) + nn(lo[par], h_ref[:own, ln]))

    def ahead(l, carry):
        def keep(par, n, out):
            for c in range(3):
                at = pl.ds(pl.multiple_of((2 * (3 * l + c) + par) * R, 8), main)
                for k in range(2):
                    uz[2 * n + k, at, :] = out[c * main:(c + 1) * main, 128 * k:128 * (k + 1)]
        for c in range(3):
            x3[c * main:c * main + rows, :] = xb[3 * l + c]
        samples(x3[...], tab_h.at[l], tab_l.at[l], keep)
        return carry

    lax.fori_loop(0, 2, ahead, 0)

    @pl.when(has_next)
    def _():
        for copy in to_prev[3:]:
            copy.wait_recv()

    @pl.when(jnp.logical_not(has_next))
    def _():
        rh[...] = jnp.zeros_like(rh)
        rpack[...] = jnp.zeros_like(rpack)
        ring[:, main:] = jnp.zeros((2, HR, 128), f32)
    for copy in to_ring:
        copy.wait_recv()
    near = []
    for c in range(3):
        low, upper = ring[1], ring[0]
        if c:
            low, upper = pltpu.roll(low, 128 - halo * c, 1), pltpu.roll(upper, 128 - halo * c, 1)
        hh, hl = split(jnp.concatenate([low, upper], axis=1))
        he = (nn(hh, s1_ref[...]) + nn(hl, s2_ref[...])).astype(bf16)
        near += [he[:, :128], he[:, 128:]]
    near = jnp.concatenate(near, axis=0)
    for n in range(2 * W // 256):
        out = nn(near, t3_ref[1, :, 256 * n:256 * (n + 1)])
        for k in range(2):
            ln = slice(128 * k, 128 * (k + 1))
            for i in range(6):
                uz[2 * n + k, (6 + i) * R:(6 + i) * R + main, :] += out[i * R:i * R + main, ln]
                uz[2 * n + k, (6 + i) * R + main:(7 + i) * R, :] = out[i * R + main:(i + 1) * R, ln]

    for copy, forward in zip(mod_got, mod_pass):
        copy.wait_recv()
        forward.start()

    @pl.when(has_next)
    def _():
        for copy in to_prev[:3]:
            copy.wait_recv()
    count = edge - 1
    for l, (h_ref, l_ref) in enumerate(tables):
        def keep(par, n, out, l=l):
            for c in range(3):
                at = (2 * (3 * l + c) + par) * R + main
                for k in range(2):
                    ln = slice(128 * k, 128 * (k + 1))
                    some, one = out[c * count:(c + 1) * count, ln], out[3 * count + 3 * l + c:3 * count + 3 * l + c + 1, ln]
                    if l:
                        some, one = some + uz[2 * n + k, at:at + count, :], one + uz[2 * n + k, at + count:at + edge, :]
                    uz[2 * n + k, at:at + count, :] = some
                    uz[2 * n + k, at + count:at + edge, :] = one
        x = jnp.concatenate([rh[3 * l:3 * l + 3].reshape(3 * count, lanes), rpack[...]], axis=0)
        samples(x, h_ref, l_ref, keep)
    @pl.when(me == nf - 1)
    def _():
        for c in range(3):
            for par in range(2):
                spot = 3 * halo + 2 * c + par
                column = ring[0, :, spot:spot + 1]
                at = (2 * c + par) * R
                for b in range(blocks):
                    uz[b, at:at + R, :] += column * nyq_ref[0:1, 128 * b:128 * (b + 1)]

    loads[2].wait()
    near_got.wait_recv()
    for copy in pass_got:
        copy.wait_recv()
    loads[5].wait()
    modx[...] = jnp.zeros_like(modx)
    for r in range(21):
        for d in range(nf):
            ln = slice(128 * d, 128 * d + modr.shape[4])
            modx[r, :BASIS, ln] = modr[d, r, :, 0, :] * wrow_ref[0:1, ln]

    row_nodes, row_lanes = nodes // count_a, nf * 128 // count_a
    pairs_each = -(-11 // (2 * blocks))

    def moduli_pairs(ts):
        spread_out = []
        for t in ts:
            rows_two = []
            for k in range(2):
                h, lo = split(modx[2 * t + k])
                rows_two += [h, h, lo, jnp.zeros_like(h)]
            spread_out.append(jnp.concatenate(rows_two, axis=0))
        turned = []
        for ea in range(count_a):
            ln = slice(ea * row_lanes, (ea + 1) * row_lanes)
            for t, two in zip(ts, spread_out):
                mt = nt(perm_ref[ea * row_nodes:(ea + 1) * row_nodes, ln], two[:, ln]).astype(bf16)
                turned += [(t, k, ea, mt[:, 128 * k:128 * (k + 1)]) for k in range(2)]
        out = nn(jnp.concatenate([mt for _, _, _, mt in turned], axis=0), a3_ref[...])
        for i, (t, k, ea, _) in enumerate(turned):
            at = pl.multiple_of((2 * t + k) * nodes + ea * row_nodes, 8)
            cs[pl.ds(at, row_nodes), :] = out[i * row_nodes:(i + 1) * row_nodes]

    def point(a, j):
        p = wide * a + j
        return p % 2, p // 2 + (hrow if a == 4 * count_a else 0)

    def strain_step(t, carry):
        l, blk = t // blocks, t % blocks
        blk_z = blocks + blk

        def grid(c, ea, at_blk):
            out = []
            for i in range(5):
                row = []
                for j in range(5):
                    par, r = point(4 * ea + i, j)
                    at = (2 * (3 * l + c) + par) * R + r
                    row.append(uz[at_blk, pl.ds(at, 8, stride=2), :])
                out.append(row)
            return out

        def put(v, ea, i, j, value):
            row = v * nodes + ((ea * 5 + i) * 5 + j) * 8
            es[l, blk, row:row + 8, :] = value

        for ea in range(count_a):
            rad = lambda i, j: rad_ref[((ea * 5 + i) * 5 + j) * 8:((ea * 5 + i) * 5 + j) * 8 + 8, :]
            cols = lambda u: [[row[j] for row in u] for j in range(5)]
            u = grid(0, ea, blk)
            for j, col in enumerate(cols(u)):
                for i, v in enumerate(line(derive, col)):
                    put(0, ea, i, j, v)
            shear = [line(derive, row) for row in u]
            u = grid(1, ea, blk)
            for j, col in enumerate(cols(u)):
                for i, v in enumerate(line(derive, col)):
                    put(5, ea, i, j, v + shear[i][j])
            for i, row in enumerate(u):
                for j, v in enumerate(line(derive, row)):
                    put(1, ea, i, j, v)
            u = grid(2, ea, blk)
            z = grid(0, ea, blk_z)
            for j, col in enumerate(cols(u)):
                for i, v in enumerate(line(derive, col)):
                    put(4, ea, i, j, v + rad(i, j) * z[i][j])
            z = grid(1, ea, blk_z)
            for i, row in enumerate(u):
                for j, v in enumerate(line(derive, row)):
                    put(3, ea, i, j, v + rad(i, j) * z[i][j])
            z = grid(2, ea, blk_z)
            for i in range(5):
                for j in range(5):
                    put(2, ea, i, j, rad(i, j) * z[i][j])
        moduli_pairs([t * pairs_each + k for k in range(pairs_each)])
        return carry

    lax.fori_loop(0, 2 * blocks, strain_step, 0)

    def node_step(t, carry):
        row = pl.multiple_of(t * 8, 8)
        at = lambda v: pl.ds(pl.multiple_of(v * nodes + row, 8), 8)

        def add(sums, v, term):
            sums[v] = term if sums[v] is None else sums[v] + term

        def one(ce, els):
            fw = [[es[0, el, at(v), :] for v in range(6)] for el in els]
            ad = [[es[1, el, at(v), :] for v in range(6)] for el in els]
            sf = [[None] * 6 for _ in els]
            sa = [[None] * 6 for _ in els]
            for r, (v, w) in enumerate(PAIRS):
                c = cs[at(r), ce]
                total = None
                for f, a, tf, ta in zip(fw, ad, sf, sa):
                    add(tf, v, c * f[w])
                    add(ta, v, c * a[w])
                    if v != w:
                        add(tf, w, c * f[v])
                        add(ta, w, c * a[v])
                        prod = f[v] * a[w] + f[w] * a[v]
                    else:
                        prod = f[v] * a[v]
                    total = prod if total is None else total + prod
                ps[at(r), ce] = total
            for el, tf, ta in zip(els, sf, sa):
                for v in range(6):
                    es[0, el, at(v), :] = tf[v]
                    es[1, el, at(v), :] = ta[v]

        for b in range(nb):
            one(slice(128 * b, 128 * b + 128),
                [b, nb + b])
        one(slice(128 * nb, 128 * nb + 128), [2 * nb])
        return carry

    lax.fori_loop(0, nodes // 8, node_step, 0, unroll=2)

    each = -(-21 // (2 * blocks))

    def project(r):
        ph, plo = split(ps[pl.ds(pl.multiple_of(r * nodes, 8), nodes), :])
        both = nt(aa_ref[...], ph)
        accb[r] = both[:32] + both[32:] + nt(aa_ref[:32], plo)

    def force_step(t, carry):
        l, blk = t // blocks, t % blocks
        blk_z = blocks + blk
        top = lax.broadcasted_iota(jnp.int32, (8, 128), 0) == 0

        def get(v, ea, i, j):
            row = v * nodes + ((ea * 5 + i) * 5 + j) * 8
            return es[l, blk, row:row + 8, :]

        def store(c, a, row, at_blk):
            def where(j):
                par, r = point(a, j)
                return (2 * (3 * l + c) + par) * R + r
            for j in range(1, 4):
                uz[at_blk, pl.ds(where(j), 8, stride=2), :] = row[j]
            back = pltpu.roll(row[4], 1, 0)
            uz[at_blk, pl.ds(where(0), 8, stride=2), :] = row[0] + jnp.where(top, 0.0, back)
            uz[at_blk, pl.ds(where(4) + 14, 1), :] = row[4][7:8]

        beyond = wide * (4 * count_a + 1)
        for c in range(3):
            held, held_z = None, None
            spare = (2 * (3 * l + c) + beyond % 2) * R + beyond // 2 + hrow
            for b in (blk, blk_z):
                uz[b, pl.ds(spare, 1), :] = jnp.zeros((1, 128), f32)
            for ea in range(count_a):
                rad = lambda i, j: rad_ref[((ea * 5 + i) * 5 + j) * 8:((ea * 5 + i) * 5 + j) * 8 + 8, :]
                cols = [line(derive.T, [get(PART_A[c], ea, i, j) for i in range(5)]) for j in range(5)]
                for i in range(5):
                    row = line(derive.T, [get(PART_B[c], ea, i, j) for j in range(5)])
                    row = [row[j] + cols[j][i] for j in range(5)]
                    row_z = [rad(i, j) * get(PART_P[c], ea, i, j) for j in range(5)]
                    if i == 0 and held is not None:
                        row = [p + q for p, q in zip(row, held)]
                        row_z = [p + q for p, q in zip(row_z, held_z)]
                    if i == 4 and ea + 1 < count_a:
                        held, held_z = row, row_z
                    else:
                        store(c, 4 * ea + i, row, blk)
                        store(c, 4 * ea + i, row_z, blk_z)
        for k in range(each):
            project(t * each + k)
        return carry

    lax.fori_loop(0, 2 * blocks, force_step, 0)
    h, lo = split(accb[:21].reshape(21 * 32, nodes))
    for ea in range(count_a):
        q, ln = slice(ea * row_nodes, (ea + 1) * row_nodes), slice(ea * row_lanes, (ea + 1) * row_lanes)
        part = (nn(h[:, q], perm_ref[q, ln]) + nn(lo[:, q], perm_ref[q, ln])) * krow_ref[0:1, ln]
        for k in range(nf // count_a):
            for r in range(21):
                d = ea * (nf // count_a) + k
                kb[d % 2, d // 2, r * BASIS:(r + 1) * BASIS, :] = \
                    part[32 * r:32 * r + BASIS, 128 * k:128 * k + kb.shape[3]]
    k_near.start()

    def interleave(both):
        out = []
        for b in range(lane_blocks):
            ln = slice(128 * b, 128 * (b + 1))
            h, lo = split(jnp.concatenate([both[0][:, ln], both[1][:, ln]], axis=1))
            out.append(nt(h, s_ref[...]) + nt(lo, s_ref[...]))
        return jnp.concatenate(out, axis=1)

    def turn_back(parts, l, with_edge):
        h_ref, l_ref = tables[1 - l]
        if not with_edge:
            both = []
            for part in parts:
                h, lo = split(part)
                both.append(nt(h, h_ref[:own]) + nt(h, l_ref[:own]) + nt(lo, h_ref[:own]))
            return interleave(both), None
        count = parts[0].shape[0]
        h, lo = split(jnp.concatenate(parts, axis=0))
        cut = lambda v: [v[:count], v[count:]]
        out = interleave(cut(nt(h, h_ref[:own]) + nt(h, l_ref[:own]) + nt(lo, h_ref[:own])))
        edge_h, edge_l = cut(nt(h, t3_ref[1 - l])), cut(nt(lo, t3_ref[1 - l]))
        h, lo = split(jnp.concatenate(edge_h, axis=1))
        side = nt(h, s1_ref[...]) + nt(lo, s1_ref[...])
        h, lo = split(jnp.concatenate(edge_l, axis=1))
        return out, side + nt(h, s2_ref[...]) + nt(lo, s2_ref[...])

    def spread(side, c):
        low, high = side[:, :128], side[:, 128:]
        return (pltpu.roll(low, halo * c, 1), pltpu.roll(high, halo * c, 1)) if c else (low, high)

    def read(lc, par, start, count):
        at = (2 * lc + par) * R + start
        return jnp.concatenate([uz[b, at:at + count, :] for b in range(2 * blocks)], axis=1)

    high = jnp.zeros((R, 128), f32)
    lane_r = lax.broadcasted_iota(jnp.int32, (R, 128), 1)
    for c in range(3):
        for par in range(2):
            at = (2 * (3 + c) + par) * R
            terms = None
            for b in range(blocks):
                term = uz[b, at:at + R, :] * nyq_ref[0:1, 128 * b:128 * (b + 1)]
                terms = term if terms is None else terms + term
            value = jnp.sum(terms, axis=1, keepdims=True) * is_last
            high = jnp.where(lane_r == 3 * halo + 2 * c + par, value, high)
    spill[0] = jnp.zeros((R, 128), f32)
    spill[1] = high

    for l in range(2):
        parts = [jnp.concatenate([read(3 * l + c, par, main, HR) for c in range(3)], axis=0) for par in range(2)]
        out, side = turn_back(parts, l, l == 0)
        for c in range(3):
            edge_f[3 * l + c] = out[c * HR:c * HR + count]
            edge_p[3 * l + c:3 * l + c + 1, :] = out[c * HR + count:c * HR + edge]
        if l == 0:
            for c in range(3):
                for way, value in enumerate(spread(side[c * HR:(c + 1) * HR], c)):
                    spill[way, main:] += value

    edge_p[6:, :] = jnp.zeros((2, lanes), f32)

    @pl.when(has_next)
    def _():
        for copy in to_next:
            copy.start()
    k_near.wait_recv()
    k_near.wait_send()
    kb[odd] += kr[...]
    for copy in k_far:
        copy.start()
    for c in range(3):
        out, side = turn_back([read(c, par, 0, main) for par in range(2)], 0, True)
        force[c] = out[:rows]
        for way, value in enumerate(spread(side, c)):
            spill[way, :main] += value
    for copy in to_spill:
        copy.start()

    def adjoint_back(c, carry):
        at = [pl.ds(pl.multiple_of((2 * (3 + c) + par) * R, 8), main) for par in range(2)]
        parts = [jnp.concatenate([uz[b, a, :] for b in range(2 * blocks)], axis=1) for a in at]
        out, _ = turn_back(parts, 1, False)
        force[3 + c] = out[:rows]
        return carry

    lax.fori_loop(0, 3, adjoint_back, 0)

    lane_m = lax.broadcasted_iota(jnp.int32, (rows, 128), 1)

    def gather(start, count):
        for c in range(3):
            up_turned = rspill[1, start:start + count]
            up_turned = pltpu.roll(up_turned, 128 - halo * c, 1) if c else up_turned
            force[c, :count, :128] += jnp.where(lane_m[:count] < halo, up_turned, 0.0)
            low_turned = pltpu.roll(rspill[0, start:start + count], (128 - halo * (c + 1)), 1)
            force[c, :count, lanes - 128:] += jnp.where(lane_m[:count] >= 128 - halo, low_turned, 0.0)
            top_turned = pltpu.roll(rspill[1, start:start + count], 128 - 3 * halo - 2 * c + 2, 1)
            force[3 + c, :count, :128] += jnp.where((lane_m[:count] >= 2) & (lane_m[:count] < 4), top_turned, 0.0)

    @pl.when(has_prev)
    def _():
        for copy in to_next:
            copy.wait_recv()
        force[:, :edge - 1] += rm[...]
        for lc in range(6):
            force[lc, edge - 1:edge, :] += rmp[lc:lc + 1, :]
        gather(main, edge)
    for copy in to_spill:
        copy.wait_recv()
    gather(0, rows)
    mass = jnp.concatenate([mass_ref[:rows]] * (lanes // 128), axis=1)
    for c in range(3):
        f_ref[c] = mass * force[c]
        a_ref[c] = mass * force[3 + c]
    for copy in k_far:
        copy.wait_recv()
    total = kb[odd, mine]
    for s in range(half - 1):
        total = total + ks[s]
    for r in range(21):
        k_ref[r, :, 0, :] = total[r * BASIS:(r + 1) * BASIS]

    @pl.when(has_prev)
    def _():
        for copy in to_prev:
            copy.wait_send()

    @pl.when(has_next)
    def _():
        for copy in to_next:
            copy.wait_send()
    for copy in to_ring + to_spill + mod_far + [mod_near] + mod_pass + k_far:
        copy.wait_send()


def body(forward_now, forward_last, adjoint_now, adjoint_last, moduli, inv_radius, inv_mass):
    derive, weights = gll_tables()
    wide = 4 * EB + 1
    nf = lax.axis_size("fourier")
    nm = lax.axis_size("meridian")
    me = lax.axis_index("fourier")
    comps, rows, lanes = forward_now.shape
    local = lanes // 2
    total = local * nf
    orders = local // 2
    own = -(-local // 128) * 128
    row_count = 2 * rows // wide
    count_a = row_count // 4
    nodes_mine = moduli.shape[3]
    nodes = nodes_mine * nf
    edge = (wide + 1) // 2
    start = -(-rows // 8) * 8
    R = start + HR
    n, nb = sample_count(orders)
    W = 256 * nb + 128
    halo = 4 * ORD

    flat = jax.ShapeDtypeStruct((21 * BASIS, nodes_mine), f32)

    inner, first, last, halo_last = block_tables(orders, own)
    drop = np.zeros_like(first[:32])
    drop[:] = with_turned(np.where(np.arange(32)[:, None] == 1, -inner[:32, :W], 0.0))
    fixes = np.concatenate([first[:32], drop, last[local - 16:local], first[own:], last[own:], halo_last[own:]], axis=0)

    rows_a = basis_rows(orders)
    bh, bl = split_host(rows_a)
    a3 = np.zeros((128, rows_a.shape[1]), bf16)
    a3[0:BASIS], a3[32:32 + BASIS], a3[64:64 + BASIS] = bh, bl, bh
    aa = np.zeros((64, rows_a.shape[1]), bf16)
    aa[0:BASIS], aa[32:32 + BASIS] = bh, bl
    perm = np.zeros((nodes, nf * 128), np.float32)
    wrow = np.zeros((8, nf * 128), np.float32)
    for ea in range(count_a):
        for eb in range(EB):
            for ij in range(25):
                q = (ea * EB + eb) * 25 + ij
                spot = (q // nodes_mine) * 128 + q % nodes_mine
                perm[(ea * 25 + ij) * EB + eb, spot] = 1.0
                wrow[:, spot] = weights[ij]
    cfg = (nf, nm, own, R, wide, count_a, nodes, nb, start - rows, edge, orders, derive)
    vmem = pl.BlockSpec(memory_space=pltpu.VMEM)
    hbm = pl.BlockSpec(memory_space=pl.ANY)
    CW = rows_a.shape[1]
    steps = 2 * (2 * nb + 1)
    pairs, terms = -(-11 // steps) * steps, -(-21 // steps) * steps
    copies = 13 + 2 * nf
    field = jax.ShapeDtypeStruct((comps, rows, lanes), f32)
    force_f, force_a, sums = pl.pallas_call(
        functools.partial(core, cfg),
        out_shape=(field, field, jax.ShapeDtypeStruct(moduli.shape, f32)),
        in_specs=[hbm] * 6 + [vmem] * 7,
        out_specs=(vmem, vmem, vmem),
        scratch_shapes=[pltpu.VMEM((2 * W // 128, 4 * comps * R, 128), f32), pltpu.VMEM((2, W // 128, 6 * nodes, 128), f32),
                        pltpu.VMEM((2 * pairs * nodes, CW), f32), pltpu.VMEM((terms * nodes, CW), f32),
                        pltpu.VMEM((terms, 32, nodes), f32), pltpu.VMEM((lanes * 128 // own, 256), bf16),
                        pltpu.VMEM((256, 256), bf16), pltpu.VMEM((256, 256), bf16),
                        pltpu.VMEM((2, 128, 2 * W), bf16),
                        pltpu.VMEM((2 * comps, rows, lanes), f32),
                        pltpu.VMEM((nf,) + moduli.shape, f32), pltpu.VMEM((2 * pairs, 32, nf * 128), f32),
                        pltpu.VMEM((2 * comps, edge - 1, lanes), f32), pltpu.VMEM((2, R - HR, 128), f32),
                        pltpu.VMEM((2, R, 128), f32), pltpu.VMEM((2 * comps, rows, lanes), f32),
                        pltpu.VMEM((2 * comps, edge - 1, lanes), f32), pltpu.VMEM((2 * comps, edge - 1, lanes), f32),
                        pltpu.VMEM((2, R, 128), f32), pltpu.VMEM((2, R, 128), f32),
                        pltpu.VMEM((2, nf // 2) + flat.shape, f32), pltpu.VMEM((nf // 2,) + flat.shape, f32),
                        pltpu.VMEM((max(nf // 2 - 1, 1),) + flat.shape, f32),
                        pltpu.VMEM((nodes, 128), f32), pltpu.VMEM((-(-rows // 8) * 8, 128), f32),
                        pltpu.VMEM((2, own + halo, 2 * W), bf16), pltpu.VMEM((2, own + halo, 2 * W), bf16),
                        pltpu.VMEM(inner.shape, f32), pltpu.VMEM(fixes.shape, f32), pltpu.VMEM(perm.shape, bf16),
                        pltpu.VMEM((8, lanes), f32), pltpu.VMEM((8, lanes), f32),
                        pltpu.VMEM((8, lanes), f32), pltpu.VMEM((8, lanes), f32), pltpu.VMEM((comps * start, lanes), f32),
                        pltpu.SemaphoreType.DMA((6,)), pltpu.SemaphoreType.DMA((copies,)),
                        pltpu.SemaphoreType.DMA((copies,))],
        compiler_params=pltpu.CompilerParams(vmem_limit_bytes=60 * 1024 * 1024, collective_id=0,
                                             has_side_effects=True),
    )(forward_now, adjoint_now, moduli, jnp.asarray(inner), jnp.asarray(fixes),
      jnp.asarray(perm.astype(bf16)), inv_radius.reshape(1, nodes), inv_mass.reshape(1, 2 * rows), jnp.asarray(a3), jnp.asarray(aa), jnp.asarray(wrow * (2.0 / n)),
      jnp.asarray(wrow * (kernel_weight * 2.0 * total / n)),
      jnp.asarray(np.broadcast_to(0.5 * waves(orders)[0][orders + ORD], (8, W)).astype(np.float32)))
    return 2.0 * forward_now - forward_last - force_f, 2.0 * adjoint_now - adjoint_last - force_a, sums


def solution(mesh):
    field = P(None, "meridian", "fourier")
    grid = P(None, None, "meridian", "fourier")
    in_specs = (field, field, field, field, grid, P("meridian"), P("meridian"))
    return jax.shard_map(body, mesh=mesh, in_specs=in_specs, out_specs=(field, field, grid),
                         check_vma=False)
```
